32 devices in a mesh: dp: 32 (over z, y, x, core).
Axes of the slice: x: 2, y: 2, z: 4, core: 2. Of those that a mesh axis runs over, the one named last changes fastest.
Arguments:
- inputs: bfloat16 [32, 1024, 768], P('dp'), may hold values from -6 to 6
- cotangent: bfloat16 [32, 1024, 768], P('dp'), may hold values from -6 to 6
- routes: int32 [32, 1024, 1], P('dp'), may hold values from 0 to 31; in each aligned block of 1024 rows (0 to 1023, 1024 to 2047, ..., all dimensions but the last counted through in order) at most 64 rows name the same one
- segments: int32 [32, 1024], P('dp'), may hold values from 0 to 7, never falling along the last dimension, each value on 1 to 512 neighbouring positions
- qkv_weight: float32 [768, 2304], P('dp'), may hold values from -0.21875 to 0.21875
- query_bias: float32 [768], P('dp'), may hold values from -1 to 1
- value_bias: float32 [768], P('dp'), may hold values from -0.5 to 0.5
- out_weight: float32 [768, 768], P('dp'), may hold values from -0.625 to 0.625
- out_bias: float32 [768], P('dp'), may hold values from -0.5 to 0.5
- attn_gain: float32 [768], P('dp'), may hold values from 0.5 to 1.5
- attn_shift: float32 [768], P('dp'), may hold values from -0.5 to 0.5
- moe_gain: float32 [768], P('dp'), may hold values from 0.5 to 1.5
- moe_shift: float32 [768], P('dp'), may hold values from -0.5 to 0.5
- router_weight: float32 [768, 32], P('dp'), may hold values from -0.15625 to 0.15625
- expert_in: float32 [32, 768, 3072], P('dp'), may hold values from -0.21875 to 0.21875
- expert_in_bias: float32 [32, 3072], P('dp'), may hold values from -0.5 to 0.5
- expert_out: float32 [32, 3072, 768], P('dp'), may hold values from -0.3125 to 0.3125
- expert_out_bias: float32 [32, 768], P('dp'), may hold values from -0.5 to 0.5
Outputs:
- output: bfloat16 [32, 1024, 768], P('dp')
- grad_inputs: float32 [32, 1024, 768], P('dp')
- grad_qkv_weight: float32 [768, 2304], P('dp')
- grad_query_bias: float32 [768], P('dp')
- grad_value_bias: float32 [768], P('dp')
- grad_out_weight: float32 [768, 768], P('dp')
- grad_out_bias: float32 [768], P('dp')
- grad_attn_gain: float32 [768], P('dp')
- grad_attn_shift: float32 [768], P('dp')
- grad_moe_gain: float32 [768], P('dp')
- grad_moe_shift: float32 [768], P('dp')
- grad_router_weight: float32 [768, 32], P('dp')
- grad_expert_in: float32 [32, 768, 3072], P('dp')
- grad_expert_in_bias: float32 [32, 3072], P('dp')
- grad_expert_out: float32 [32, 3072, 768], P('dp')
- grad_expert_out_bias: float32 [32, 768], P('dp')
The draws below stay inside these ranges and needn't reach their ends.
Inputs may be any that keep to these rules, and one draw needn't show every extreme that they name: `routes`: each token names one expert; among the tokens of one device no expert is named more than 64 times, a bound that some block reaches. `segments`: document numbers never fall along a row; a document holds at most 512 tokens.
All inputs are finite; a program needn't handle non-finite values.
Results may differ from the reference program's by a relative error of at most 0.015.
Values may be sent and summed in bfloat16 or wider, within the bound.
No kernel may reach another device: no remote copies, remote signals or barrier semaphores. Data moves between devices by JAX's collectives and lax.ppermute only.
A program may use at most 384 MiB of HBM per device.

```python
import math
import jax
import jax.numpy as jnp
import numpy as np
from jax import lax

D = 768
HEADS = 12
HEAD_DIM = 64
FF = 3072
LEN = 1024
SEGS = 8
TOK_DEV = 1024
SEQS = 32
TOKENS = 32768
EXPERTS = 32
CAP = 64
N_DP = 32


def with_spikes(entries, stream_key, source, target, parts, factor):
    owner, partner = [(jnp.arange(entries.shape[position]) // (entries.shape[position] // parts)).reshape([-1 if axis == position else 1 for axis in range(entries.ndim)]) for position in (source, target)]
    chosen = jax.random.permutation(stream_key, parts)[partner]
    strong = (owner == chosen) | (owner == (partner + parts // 2) % parts)
    return jnp.where(strong, factor * entries, entries)


def shard_levels(key, dims, cuts, smallest, top_value):
    factor_of = 1.0
    for position, parts in cuts:
        draws = jax.random.uniform(jax.random.fold_in(jax.random.fold_in(key, 6), position), (parts,), jnp.float32, smallest / len(cuts), top_value / len(cuts))
        factor_of = factor_of * jnp.repeat(jnp.exp(draws), dims[position] // parts).reshape((-1,) + (1,) * (len(dims) - 1 - position))
    return factor_of


def length_profile(count, total, bound, skew):
    portions = [(1 << 20) // math.isqrt(rank ** skew) + 1 for rank in range(2, count + 1)]
    surplus, counts = total - bound - (count - 1), [1] * (count - 1)
    while surplus > 0:
        candidates = [i for i in range(count - 1) if counts[i] < bound]
        mass, left = sum([portions[i] for i in candidates]), surplus
        for i in candidates:
            extra = min(bound - counts[i], max(1, left * portions[i] // mass), surplus)
            counts[i] = counts[i] + extra
            surplus = surplus - extra
    return np.array([bound] + counts)


def uneven_parts(key, count, total, limit, slope):
    if count == 2:
        one = jax.random.randint(key, (), max(1, total - limit), min(limit, total - 1) + 1)
        return jnp.stack([one, total - one])
    sizes = jnp.asarray(length_profile(count, total, limit, slope), jnp.int32)
    pairs = (count - 1) // 2
    giver, sink = sizes[1:1 + 2 * pairs:2], sizes[2:2 + 2 * pairs:2]
    margin = jnp.minimum(giver - 1, limit - sink)
    moved = jax.random.randint(jax.random.fold_in(key, 1), (pairs,), 0, 1 << 20) % (margin + 1)
    sizes = sizes.at[1:1 + 2 * pairs:2].set(giver - moved).at[2:2 + 2 * pairs:2].set(sink + moved)
    return sizes[jax.random.permutation(jax.random.fold_in(key, 2), count)]


def shared_out(rng, own, number, rows, number_of, top, limit, skew):
    sequence = jax.random.permutation(rng, number_of)
    heavy_load, ordinary = load_shares(number_of, rows * top, limit, skew, True), load_shares(number_of, rows * top, limit, skew, False)
    places = jnp.arange(number_of)

    def named(lengths, rotation):
        used = int((lengths > 0).sum())
        fixed = max(1, used // 4)
        shifted = fixed + (places - fixed + rotation * (used - fixed)) % max(1, number_of - fixed)
        return jnp.zeros((number_of,), jnp.int32).at[sequence[jnp.where(places < fixed, places, shifted)]].set(jnp.asarray(lengths, jnp.int32))

    lengths = jnp.where(number % 4 == 0, named(heavy_load, number // 4), named(ordinary, number - number // 4 - 1))
    mixed = jax.random.permutation(jax.random.fold_in(own, 3), number_of)
    donor, receiver = mixed[0:number_of // 2 * 2:2], mixed[1:number_of // 2 * 2:2]
    slack = jnp.minimum(lengths[donor] - 1, limit - lengths[receiver]) // 2
    slack = jnp.where((donor == sequence[0]) | (receiver == sequence[0]) | (lengths[receiver] == 0), 0, jnp.maximum(slack, 0))
    shifted = jax.random.randint(jax.random.fold_in(own, 4), (number_of // 2,), 0, 1 << 20) % (slack + 1)
    lengths = lengths.at[donor].add(-shifted).at[receiver].add(shifted)
    items = jnp.searchsorted(jnp.cumsum(lengths), jnp.arange(rows * top), side="right").astype(jnp.int32)
    listing = items.reshape(top, rows).T
    listing = listing[jax.random.permutation(jax.random.fold_in(own, 1), rows)]
    rotation = jax.random.randint(jax.random.fold_in(own, 2), (rows, 1), 0, top)
    return jnp.take_along_axis(listing, (jnp.arange(top)[None, :] + rotation) % top, axis=1)


def load_shares(amount, total, limit, skew, full):
    portions = [(1 << 20) // math.isqrt(grade ** skew) + 1 for grade in range(1, amount + 1)]
    largest = limit if full else min(limit, max(-(-total // amount), total * portions[0] // sum(portions)))
    least = 1 if total - largest >= amount - 1 else 0
    counts, surplus = [largest] + [least] * (amount - 1), total - largest - least * (amount - 1)
    while surplus > 0:
        movable = [i for i in range(1, amount) if counts[i] < largest] or [i for i in range(1, amount) if counts[i] < limit]
        whole, left = sum([portions[i] for i in movable]), surplus
        for i in movable:
            more = min(limit - counts[i], max(1, left * portions[i] // whole), surplus)
            counts[i] = counts[i] + more
            surplus = surplus - more
    return np.array(counts)


def normal_values(rng, extent, deviation, limit, cuts=(), held_as=jnp.bfloat16):
    values = deviation * jax.random.normal(rng, extent, jnp.float32)
    if cuts:
        values = values * shard_levels(rng, extent, cuts, -0.22, 0.18)
    return jnp.clip(values, -limit, limit).astype(held_as)


def noise_with(rng, extent, deviation, limit, cuts, heavy, kind=jnp.bfloat16):
    drawn = deviation * jax.random.normal(rng, extent, jnp.float32)
    if cuts:
        drawn = drawn * shard_levels(rng, extent, cuts, -0.22, 0.18)
    return jnp.clip(with_spikes(drawn, jax.random.fold_in(rng, 3), *heavy), -limit, limit).astype(kind)


def setup_inputs(seed: int = 0) -> dict:
    seeds = jax.random.split(jax.random.key(seed), 19)
    inputs = normal_values(seeds[0], (SEQS, LEN, D), 1.0, 6.0, ((0, 32),))
    cotangent = noise_with(seeds[1], (SEQS, LEN, D), 1.0, 6.0, ((0, 32),), (0, 2, 32, 2.75))
    routes_keys = jax.random.split(jax.random.fold_in(seeds[2], 1), SEQS * LEN // TOK_DEV)
    routes_turns = jax.random.permutation(jax.random.fold_in(seeds[2], 3), SEQS * LEN // TOK_DEV)
    routes = jax.vmap(lambda own, number: shared_out(jax.random.fold_in(seeds[2], 2), own, number, TOK_DEV, EXPERTS, 1, CAP, 2))(routes_keys, routes_turns).reshape((SEQS, LEN, 1))
    segments = jax.vmap(lambda own: jnp.searchsorted(jnp.cumsum(uneven_parts(own, SEGS, LEN, LEN // 2, 2)), jnp.arange(LEN), side="right"))(jax.random.split(seeds[3], SEQS)).reshape((SEQS, LEN)).astype(jnp.int32)
    qkv_weight = normal_values(seeds[4], (D, 3 * D), D ** -0.5, 0.21875, ((0, 32),), jnp.float32)
    query_bias = normal_values(seeds[5], (D,), 0.2, 1.0, ((0, 32),), jnp.float32)
    value_bias = normal_values(seeds[6], (D,), 0.1, 0.5, ((0, 32),), jnp.float32)
    out_weight = normal_values(seeds[7], (D, D), (D // 8) ** -0.5, 0.625, ((0, 32),), jnp.float32)
    out_bias = normal_values(seeds[8], (D,), 0.1, 0.5, ((0, 32),), jnp.float32)
    attn_gain = jnp.clip(1.0 + 0.1 * jax.random.normal(seeds[9], (D,), jnp.float32), 0.5, 1.5)
    attn_shift = normal_values(seeds[10], (D,), 0.1, 0.5, ((0, 32),), jnp.float32)
    moe_gain = jnp.clip(1.0 + 0.1 * jax.random.normal(seeds[11], (D,), jnp.float32), 0.5, 1.5)
    moe_shift = normal_values(seeds[12], (D,), 0.1, 0.5, ((0, 32),), jnp.float32)
    router_weight = normal_values(seeds[13], (D, EXPERTS), (2 * D) ** -0.5, 0.15625, ((0, 32),), jnp.float32)
    expert_in = normal_values(seeds[14], (EXPERTS, D, FF), D ** -0.5, 0.21875, ((0, 32),), jnp.float32)
    expert_in_bias = normal_values(seeds[15], (EXPERTS, FF), 0.1, 0.5, ((0, 32),), jnp.float32)
    expert_out = normal_values(seeds[16], (EXPERTS, FF, D), (FF // 8) ** -0.5, 0.3125, ((0, 32),), jnp.float32)
    expert_out_bias = normal_values(seeds[17], (EXPERTS, D), 0.1, 0.5, ((0, 32),), jnp.float32)
    return dict(inputs=inputs, cotangent=cotangent, routes=routes, segments=segments, qkv_weight=qkv_weight, query_bias=query_bias, value_bias=value_bias, out_weight=out_weight, out_bias=out_bias, attn_gain=attn_gain, attn_shift=attn_shift, moe_gain=moe_gain, moe_shift=moe_shift, router_weight=router_weight, expert_in=expert_in, expert_in_bias=expert_in_bias, expert_out=expert_out, expert_out_bias=expert_out_bias)


EPSILON = 1e-05
NEG_FILL = -1000000000.0
HIGHEST = lax.Precision.HIGHEST

@jax.custom_vjp
def low(v):
    return lax.optimization_barrier(v.astype(jnp.bfloat16)).astype(jnp.float32)

@jax.custom_vjp
def low_back(v):
    return v

def low_keep(v):
    return (low(v), None)

def low_pass(kept, grad):
    return (grad,)

def back_keep(v):
    return (v, None)

def back_low(kept, grad):
    return (low(grad),)
low.defvjp(low_keep, low_pass)
low_back.defvjp(back_keep, back_low)

def norm_rows(value, gain, shift):
    mean = lax.optimization_barrier(jnp.mean(value, axis=1, keepdims=True))
    centred = value - mean
    spread = lax.optimization_barrier(jnp.mean(centred * centred, axis=1, keepdims=True))
    return centred * lax.rsqrt(spread + EPSILON) * gain + shift

def attend(item):
    queries, keys, values, segment = item
    length = queries.shape[0]
    scores = jnp.einsum('qhd,khd->hqk', queries, keys, precision=HIGHEST) * HEAD_DIM ** (-0.5)
    places = jnp.arange(length, dtype=jnp.int32)
    allowed = (segment[:, None] == segment[None, :]) & (places[None, :] <= places[:, None])
    scores = low_back(jnp.where(allowed[None], scores, NEG_FILL))
    probs = low(jax.nn.softmax(scores, axis=2))
    return jnp.einsum('hqk,khd->qhd', probs, values, precision=HIGHEST)

def run_expert(item):
    rows, weight_in, bias_in, weight_out, bias_out = item
    preact = low_back(jnp.dot(rows, weight_in, precision=HIGHEST) + bias_in)
    active = low(jax.nn.gelu(preact, approximate=False))
    return low(low_back(jnp.dot(active, weight_out, precision=HIGHEST) + bias_out))

def reference(inputs, cotangent, routes, segments, qkv_weight, query_bias, value_bias, out_weight, out_bias, attn_gain, attn_shift, moe_gain, moe_shift, router_weight, expert_in, expert_in_bias, expert_out, expert_out_bias):
    route = routes.reshape(N_DP, TOK_DEV)
    onehot = (route[:, :, None] == jnp.arange(EXPERTS, dtype=jnp.int32)[None, None, :]).astype(jnp.int32)
    slot = lax.optimization_barrier(jnp.sum(jnp.cumsum(onehot, axis=1) * onehot, axis=2)) - 1
    source = jnp.arange(N_DP, dtype=jnp.int32)[:, None]
    place = (route * (N_DP * CAP) + source * CAP + slot).reshape(TOKENS).astype(jnp.int32)
    source_row = jnp.zeros((EXPERTS * N_DP * CAP,), jnp.int32).at[place].set(jnp.arange(TOKENS, dtype=jnp.int32))
    occupied = jnp.zeros((EXPERTS * N_DP * CAP,), jnp.float32).at[place].set(1.0)
    flat_route = route.reshape(TOKENS, 1).astype(jnp.int32)

    def forward(x_in, qkv_w, query_b, value_b, out_w, out_b, attn_g, attn_s, moe_g, moe_s, router_w, exp_in, exp_in_b, exp_out, exp_out_b):
        rows_in = x_in.reshape(TOKENS, D)
        normed = low(norm_rows(rows_in, low(attn_g), low(attn_s)))
        bias = jnp.concatenate([low(query_b), jnp.zeros((D,), jnp.float32), low(value_b)])
        packed = jnp.dot(normed, low(qkv_w), precision=HIGHEST) + bias
        shape = (SEQS, LEN, HEADS, HEAD_DIM)
        queries = low(low_back(packed[:, :D])).reshape(shape)
        keys = low(low_back(packed[:, D:2 * D])).reshape(shape)
        values = low(low_back(packed[:, 2 * D:])).reshape(shape)
        mixed = lax.map(jax.checkpoint(attend), (queries, keys, values, segments))
        mixed = low(low_back(mixed.reshape(TOKENS, D)))
        hidden = rows_in + low_back(jnp.dot(mixed, low(out_w), precision=HIGHEST) + low(out_b))
        moe_in = low(norm_rows(hidden, low(moe_g), low(moe_s)))
        logits = low_back(jnp.dot(moe_in, low(router_w), precision=HIGHEST))
        gate = jax.nn.sigmoid(jnp.take_along_axis(logits, flat_route, axis=1)[:, 0])
        expert_rows = (low_back(moe_in)[source_row] * occupied[:, None]).reshape(EXPERTS, N_DP * CAP, D)
        returned = lax.map(jax.checkpoint(run_expert), (expert_rows, low(exp_in), exp_in_b, low(exp_out), exp_out_b))
        token_back = returned.reshape(EXPERTS * N_DP * CAP, D)[place]
        output = hidden + gate[:, None] * token_back
        return output.reshape(SEQS, LEN, D)
    primals = (inputs.astype(jnp.float32), qkv_weight, query_bias, value_bias, out_weight, out_bias, attn_gain, attn_shift, moe_gain, moe_shift, router_weight, expert_in, expert_in_bias, expert_out, expert_out_bias)
    output, pull = jax.vjp(forward, *primals)
    grads = pull(cotangent.astype(jnp.float32))
    return (output.astype(jnp.bfloat16), grads[0], grads[1], grads[2], grads[3], grads[4], grads[5], grads[6], grads[7], grads[8], grads[9], grads[10], grads[11], grads[12], grads[13], grads[14])
```

```python
import functools

import jax
import jax.numpy as jnp
from jax import lax
from jax.experimental import pallas as pl
from jax.experimental.pallas import tpu as pltpu
from jax.sharding import PartitionSpec as P

HEAD_DIM = 64
PAIR = 2 * HEAD_DIM
GROUPS = 3
QBLOCK = 256
MAX_DOC = 512
CHUNKS = 2
EPSILON = 1e-05
NEG_FILL = -1000000000.0
SQRT_HALF = 0.7071067811865476
INV_ROOT_TAU = 0.3989422804014327
F32 = jnp.float32
BF16 = jnp.bfloat16
VMEM_LIMIT = 56 * 1024 * 1024


def dot(a, b):
    return lax.dot_general(a, b, (((1,), (0,)), ((), ())), preferred_element_type=F32)


def dot_nt(a, b):
    return lax.dot_general(a, b, (((1,), (1,)), ((), ())), preferred_element_type=F32)


def dot_tn(a, b):
    return lax.dot_general(a, b, (((0,), (0,)), ((), ())), preferred_element_type=F32)


def params():
    return pltpu.CompilerParams(vmem_limit_bytes=VMEM_LIMIT)


def whole(shape):
    return pl.BlockSpec(shape, lambda *_: (0,) * len(shape))


def window(index):
    return max(0, index * QBLOCK - MAX_DOC), (index + 1) * QBLOCK


def iota(shape, axis):
    return lax.broadcasted_iota(jnp.int32, shape, axis)


def norm_stats(value):
    mean = jnp.mean(value, axis=1, keepdims=True)
    centred = value - mean
    spread = jnp.mean(centred * centred, axis=1, keepdims=True)
    inverse = lax.rsqrt(spread + EPSILON)
    return centred * inverse, inverse


def norm_back(grad, scaled, inverse, gain):
    inner = grad * gain
    return inverse * (
        inner
        - jnp.mean(inner, axis=1, keepdims=True)
        - scaled * jnp.mean(inner * scaled, axis=1, keepdims=True)
    )


def attend_kernel(x_ref, w_ref, b_ref, sc_ref, sr_ref, qkv_ref, mix_ref, lse_ref):
    tokens = x_ref.shape[0]
    wide = mix_ref.shape[1]
    pairs = wide // PAIR
    qkv_ref[...] = (dot(x_ref[...], w_ref[...]) + b_ref[...]).astype(BF16)
    lane = iota((QBLOCK, PAIR), 1)
    for i in range(tokens // QBLOCK):
        lo, hi = window(i)
        r0 = i * QBLOCK
        rows = slice(r0, r0 + QBLOCK)
        allowed = (sc_ref[rows, :] == sr_ref[:, lo:hi]) & (
            iota((QBLOCK, hi - lo), 1) + lo <= iota((QBLOCK, hi - lo), 0) + r0
        )
        total = jnp.zeros((QBLOCK, PAIR), F32)
        for p in range(pairs):
            q = qkv_ref[rows, p * PAIR : (p + 1) * PAIR] * jnp.asarray(HEAD_DIM**-0.5, BF16)
            k = qkv_ref[lo:hi, wide + p * PAIR : wide + (p + 1) * PAIR]
            v = qkv_ref[lo:hi, 2 * wide + p * PAIR : 2 * wide + (p + 1) * PAIR]
            outs = []
            for h in range(2):
                mine = (lane >= HEAD_DIM) if h else (lane < HEAD_DIM)
                qm = jnp.where(mine, q, jnp.zeros((), BF16))
                s = jnp.where(allowed, dot_nt(qm, k), NEG_FILL)
                top = jnp.max(s, axis=1, keepdims=True)
                e = jnp.exp(s - top)
                l = jnp.sum(e, axis=1, keepdims=True)
                outs.append(dot(e.astype(BF16), v) / l)
                total = jnp.where(lane == 2 * p + h, top + jnp.log(l), total)
            mix_ref[rows, p * PAIR : (p + 1) * PAIR] = jnp.where(
                lane < HEAD_DIM, outs[0], outs[1]
            ).astype(BF16)
        lse_ref[:, rows] = jnp.transpose(total)[: lse_ref.shape[0], :]


def attend(normed, weight, bias, seg_col, seg_row):
    tokens, width = normed.shape
    wide = weight.shape[1] // 3
    return pl.pallas_call(
        attend_kernel,
        out_shape=(
            jax.ShapeDtypeStruct((tokens, 3 * wide), BF16),
            jax.ShapeDtypeStruct((tokens, wide), BF16),
            jax.ShapeDtypeStruct((8, tokens), F32),
        ),
        compiler_params=params(),
        name="attend",
    )(normed, weight, bias, seg_col, seg_row)


def attend_back_kernel(
    qkv_ref, mix_ref, da_ref, wo_ref, lse_ref, sc_ref, sr_ref, out_ref, sum_ref, do_ref, dk_ref, dv_ref
):
    tokens = qkv_ref.shape[0]
    wide = mix_ref.shape[1]
    pairs = wide // PAIR
    do_ref[...] = dot_nt(da_ref[...], wo_ref[...]).astype(BF16)
    scale = jnp.asarray(HEAD_DIM**-0.5, BF16)
    lane = iota((QBLOCK, PAIR), 1)
    head_of = iota((8, wide), 1) // HEAD_DIM
    select = jnp.where(head_of == iota((8, wide), 0), 1.0, 0.0).astype(F32)
    delta = lax.dot_general(
        select,
        do_ref[...].astype(F32) * mix_ref[...].astype(F32),
        (((1,), (1,)), ((), ())),
        precision=lax.Precision.HIGHEST,
        preferred_element_type=F32,
    )
    for p in range(pairs):
        dk_ref[...] = jnp.zeros_like(dk_ref)
        dv_ref[...] = jnp.zeros_like(dv_ref)
        cq = slice(p * PAIR, (p + 1) * PAIR)
        ck = slice(wide + p * PAIR, wide + (p + 1) * PAIR)
        cv = slice(2 * wide + p * PAIR, 2 * wide + (p + 1) * PAIR)
        for i in range(tokens // QBLOCK):
            lo, hi = window(i)
            r0 = i * QBLOCK
            rows = slice(r0, r0 + QBLOCK)
            allowed = (sc_ref[lo:hi, :] == sr_ref[:, rows]) & (
                iota((hi - lo, QBLOCK), 0) + lo <= iota((hi - lo, QBLOCK), 1) + r0
            )
            q = qkv_ref[rows, cq] * scale
            k = qkv_ref[lo:hi, ck]
            v = qkv_ref[lo:hi, cv]
            g = do_ref[rows, cq]
            dq = jnp.zeros((QBLOCK, PAIR), F32)
            for h in range(2):
                mine = (lane >= HEAD_DIM) if h else (lane < HEAD_DIM)
                qm = jnp.where(mine, q, jnp.zeros((), BF16))
                gm = jnp.where(mine, g, jnp.zeros((), BF16))
                head = 2 * p + h
                s = jnp.where(allowed, dot_nt(k, qm), NEG_FILL)
                probs = jnp.exp(s - lse_ref[head : head + 1, rows])
                dv_ref[lo:hi, :] += dot(probs.astype(BF16), gm)
                ds = (probs * (dot_nt(v, gm) - delta[head : head + 1, rows])).astype(BF16)
                dk_ref[lo:hi, :] += dot(ds, qm)
                dq = jnp.where(mine, dot_tn(ds, k), dq)
            out_ref[rows, cq] = (dq * (HEAD_DIM**-0.5)).astype(BF16)
        out_ref[:, ck] = dk_ref[...].astype(BF16)
        out_ref[:, cv] = dv_ref[...].astype(BF16)
    sum_ref[...] = jnp.broadcast_to(
        jnp.sum(out_ref[...].astype(F32), axis=0, keepdims=True), sum_ref.shape
    )


def attend_back(qkv, mix, dattn, wo, lse, seg_col, seg_row):
    tokens, wide = mix.shape
    return pl.pallas_call(
        attend_back_kernel,
        out_shape=(
            jax.ShapeDtypeStruct((tokens, 3 * wide), BF16),
            jax.ShapeDtypeStruct((8, 3 * wide), F32),
        ),
        scratch_shapes=[
            pltpu.VMEM((tokens, wide), BF16),
            pltpu.VMEM((tokens, PAIR), F32),
            pltpu.VMEM((tokens, PAIR), F32),
        ],
        compiler_params=params(),
        name="attend_back",
    )(qkv, mix, dattn, wo, lse, seg_col, seg_row)


def project_kernel(x_ref, m0_ref, m1_ref, m2_ref, wo_ref, vec_ref, hid_ref, moe_ref):
    wide = m0_ref.shape[1]
    hidden = x_ref[...].astype(F32) + vec_ref[0:1, :]
    for g, ref in enumerate((m0_ref, m1_ref, m2_ref)):
        hidden = hidden + dot(ref[...], wo_ref[g * wide : (g + 1) * wide, :])
    hid_ref[...] = hidden
    scaled, _ = norm_stats(hidden)
    moe_ref[...] = (scaled * vec_ref[1:2, :] + vec_ref[2:3, :]).astype(BF16)


def project(x, mixes, wo, vecs):
    tokens, width = x.shape
    wide = mixes[0].shape[1]
    row = lambda n: pl.BlockSpec((QBLOCK, n), lambda i: (i, 0))
    return pl.pallas_call(
        project_kernel,
        grid=(tokens // QBLOCK,),
        in_specs=[row(width), row(wide), row(wide), row(wide), whole(wo.shape), whole(vecs.shape)],
        out_specs=(row(width), row(width)),
        out_shape=(
            jax.ShapeDtypeStruct((tokens, width), F32),
            jax.ShapeDtypeStruct((tokens, width), BF16),
        ),
        compiler_params=params(),
        name="project",
    )(x, *mixes, wo, vecs)


def pack_kernel(base, target_ref, rows_ref, out_ref):
    count = out_ref.shape[0]
    start = base + pl.program_id(0) * count
    hot = iota((count, rows_ref.shape[0]), 0) + start == target_ref[...]
    out_ref[...] = dot(jnp.where(hot, 1.0, 0.0).astype(BF16), rows_ref[...]).astype(BF16)


def pack(rows, target_row, base, count):
    tokens, width = rows.shape
    return pl.pallas_call(
        functools.partial(pack_kernel, base),
        grid=(count // 512,),
        in_specs=[whole((1, tokens)), whole(rows.shape)],
        out_specs=pl.BlockSpec((512, width), lambda i: (i, 0)),
        out_shape=jax.ShapeDtypeStruct((count, width), BF16),
        compiler_params=params(),
        name="pack",
    )(target_row, rows)


def unpack_rows(target, refs):
    base = 0
    picked = None
    for ref in refs:
        count = ref.shape[0]
        hot = iota((target.shape[0], count), 1) + base == target
        part = dot(jnp.where(hot, 1.0, 0.0).astype(BF16), ref[...])
        picked = part if picked is None else picked + part
        base += count
    return picked


def middle_kernel(*refs):
    slots = refs[:CHUNKS]
    tgt_ref, hid_ref, dy_ref, vec_ref, dhid_ref, da_ref, sum_ref = refs[CHUNKS:]
    dmoe = unpack_rows(tgt_ref[...], slots)
    scaled, inverse = norm_stats(hid_ref[...])
    dhid = dy_ref[...].astype(F32) + norm_back(dmoe, scaled, inverse, vec_ref[1:2, :])
    dhid_ref[...] = dhid
    low = dhid.astype(BF16)
    da_ref[...] = low

    @pl.when(pl.program_id(0) == 0)
    def _():
        sum_ref[...] = jnp.zeros_like(sum_ref)

    sum_ref[0:1, :] += jnp.sum(low.astype(F32), axis=0, keepdims=True)
    sum_ref[1:2, :] += jnp.sum(dmoe * scaled, axis=0, keepdims=True)
    sum_ref[2:3, :] += jnp.sum(dmoe, axis=0, keepdims=True)


def middle(slots, target_col, hidden, dy, vecs):
    tokens, width = hidden.shape
    row = lambda n: pl.BlockSpec((QBLOCK, n), lambda i: (i, 0))
    return pl.pallas_call(
        middle_kernel,
        grid=(tokens // QBLOCK,),
        in_specs=[whole(s.shape) for s in slots] + [row(1), row(width), row(width), whole(vecs.shape)],
        out_specs=(row(width), row(width), whole((8, width))),
        out_shape=(
            jax.ShapeDtypeStruct((tokens, width), F32),
            jax.ShapeDtypeStruct((tokens, width), BF16),
            jax.ShapeDtypeStruct((8, width), F32),
        ),
        compiler_params=params(),
        name="middle",
    )(*slots, target_col, hidden, dy, vecs)


def output_kernel(*refs):
    slots = refs[:CHUNKS]
    tgt_ref, route_ref, hid_ref, moe_ref, router_ref, out_ref = refs[CHUNKS:]
    logits = dot(moe_ref[...], router_ref[...])
    chosen = jnp.sum(
        jnp.where(iota(logits.shape, 1) == route_ref[...], logits, 0.0), axis=1, keepdims=True
    )
    gate = jax.nn.sigmoid(chosen)
    out_ref[...] = (hid_ref[...] + gate * unpack_rows(tgt_ref[...], slots)).astype(BF16)


def finish_output(slots, target_col, route_col, hidden, moe_in, router):
    tokens, width = hidden.shape
    row = lambda n: pl.BlockSpec((QBLOCK, n), lambda i: (i, 0))
    return pl.pallas_call(
        output_kernel,
        grid=(tokens // QBLOCK,),
        in_specs=[whole(s.shape) for s in slots]
        + [row(1), row(1), row(width), row(width), whole(router.shape)],
        out_specs=row(width),
        out_shape=jax.ShapeDtypeStruct((tokens, width), BF16),
        compiler_params=params(),
        name="finish_output",
    )(*slots, target_col, route_col, hidden, moe_in, router)


def last_kernel(d0_ref, d1_ref, d2_ref, w0_ref, w1_ref, w2_ref, x_ref, dhid_ref, vec_ref, out_ref, sum_ref):
    grad = dot_nt(d0_ref[...], w0_ref[...])
    grad = grad + dot_nt(d1_ref[...], w1_ref[...])
    grad = grad + dot_nt(d2_ref[...], w2_ref[...])
    scaled, inverse = norm_stats(x_ref[...].astype(F32))
    out_ref[...] = dhid_ref[...] + norm_back(grad, scaled, inverse, vec_ref[0:1, :])

    @pl.when(pl.program_id(0) == 0)
    def _():
        sum_ref[...] = jnp.zeros_like(sum_ref)

    sum_ref[0:1, :] += jnp.sum(grad * scaled, axis=0, keepdims=True)
    sum_ref[1:2, :] += jnp.sum(grad, axis=0, keepdims=True)


def last(dqkvs, weights, x, dhid, vecs):
    tokens, width = x.shape
    row = lambda n: pl.BlockSpec((QBLOCK, n), lambda i: (i, 0))
    return pl.pallas_call(
        last_kernel,
        grid=(tokens // QBLOCK,),
        in_specs=[row(d.shape[1]) for d in dqkvs]
        + [whole(w.shape) for w in weights]
        + [row(width), row(width), whole(vecs.shape)],
        out_specs=(row(width), whole((8, width))),
        out_shape=(
            jax.ShapeDtypeStruct((tokens, width), F32),
            jax.ShapeDtypeStruct((8, width), F32),
        ),
        compiler_params=params(),
        name="last",
    )(*dqkvs, *weights, x, dhid, vecs)


def expert_kernel(aliased, *refs):
    x_ref, dy_ref, wi_ref, bi_ref, wo_ref, vec_ref = refs[:6]
    refs = refs[6 + aliased :]
    ret_ref, dmoe_ref, act_ref, dpre_ref, arr_ref, xall_ref, gbi_ref, sum_ref = refs[:8]
    accr_ref, accg_ref = refs[8:]
    step = pl.program_id(0)

    def gate_of():
        x = x_ref[...].astype(F32)
        return jax.nn.sigmoid(jnp.sum(x * vec_ref[1:2, :], axis=1, keepdims=True))

    @pl.when(step == 0)
    def _():
        arr_ref[...] = (dy_ref[...].astype(F32) * gate_of()).astype(BF16)
        xall_ref[...] = x_ref[...]
        accr_ref[...] = jnp.broadcast_to(vec_ref[0:1, :], accr_ref.shape)
        accg_ref[...] = jnp.zeros_like(accg_ref)

    pre = dot(x_ref[...], wi_ref[...]) + bi_ref[...]
    dact = dot_nt(arr_ref[...], wo_ref[...])
    phi = 0.5 * (1.0 + lax.erf(pre * SQRT_HALF))
    act = (pre * phi).astype(BF16)
    act_ref[...] = act
    accr_ref[...] += dot(act, wo_ref[...])
    slope = phi + pre * jnp.exp(-0.5 * pre * pre) * INV_ROOT_TAU
    dpre = (dact * slope).astype(BF16)
    dpre_ref[...] = dpre
    accg_ref[...] += dot_nt(dpre, wi_ref[...])
    gbi_ref[...] = jnp.broadcast_to(
        jnp.sum(dpre.astype(F32), axis=0, keepdims=True), gbi_ref.shape
    )

    @pl.when(step == pl.num_programs(0) - 1)
    def _():
        gate = gate_of()
        ret = accr_ref[...].astype(BF16)
        ret_ref[...] = ret
        dgate = jnp.sum(dy_ref[...].astype(F32) * ret.astype(F32), axis=1, keepdims=True)
        dlogit = (dgate * gate * (1.0 - gate)).astype(BF16).astype(F32)
        dmoe_ref[...] = (
            accg_ref[...].astype(BF16).astype(F32) + dlogit * vec_ref[1:2, :]
        ).astype(BF16)
        sum_ref[...] = jnp.zeros_like(sum_ref)
        sum_ref[0:1, :] = jnp.sum(x_ref[...].astype(F32) * dlogit, axis=0, keepdims=True)
        sum_ref[1:2, :] = jnp.sum(arr_ref[...].astype(F32), axis=0, keepdims=True)


def expert_chunk(chunk, total, x, dy, w_in, b_in, w_out, vecs, kept):
    rows, width = x.shape
    hidden = w_in.shape[1]
    block = 512
    aliased = len(kept)
    any_spec = pl.BlockSpec(memory_space=pl.ANY)
    return pl.pallas_call(
        functools.partial(expert_kernel, aliased),
        grid=(hidden // block,),
        in_specs=[
            whole(x.shape),
            whole(dy.shape),
            pl.BlockSpec((width, block), lambda f: (0, f)),
            pl.BlockSpec((1, block), lambda f: (0, f)),
            pl.BlockSpec((block, width), lambda f: (f, 0)),
            whole(vecs.shape),
        ]
        + [any_spec] * aliased,
        out_specs=(
            whole((rows, width)),
            whole((rows, width)),
            pl.BlockSpec((rows, block), lambda f: (chunk, f)),
            pl.BlockSpec((rows, block), lambda f: (chunk, f)),
            pl.BlockSpec((rows, width), lambda f: (chunk, 0)),
            pl.BlockSpec((rows, width), lambda f: (chunk, 0)),
            pl.BlockSpec((8, block), lambda f: (0, f)),
            whole((8, width)),
        ),
        out_shape=(
            jax.ShapeDtypeStruct((rows, width), BF16),
            jax.ShapeDtypeStruct((rows, width), BF16),
            jax.ShapeDtypeStruct((total, hidden), BF16),
            jax.ShapeDtypeStruct((total, hidden), BF16),
            jax.ShapeDtypeStruct((total, width), BF16),
            jax.ShapeDtypeStruct((total, width), BF16),
            jax.ShapeDtypeStruct((8, hidden), F32),
            jax.ShapeDtypeStruct((8, width), F32),
        ),
        scratch_shapes=[pltpu.VMEM((rows, width), F32), pltpu.VMEM((rows, width), F32)],
        input_output_aliases={6 + i: 2 + i for i in range(aliased)},
        compiler_params=params(),
        name="expert",
    )(x, dy, w_in, b_in, w_out, vecs, *kept)


def levels_of(devices):
    side = int(round((devices // 8) ** 0.5))
    return (devices // (2 * side * side), side, side, 2)


def cyclic(devices, sizes, axis, shift):
    stride = 1
    for size in sizes[axis + 1 :]:
        stride *= size
    pairs = []
    for i in range(devices):
        at = (i // stride) % sizes[axis]
        pairs.append((i, i + ((at + shift) % sizes[axis] - at) * stride))
    return pairs


def coordinate(sizes, axis):
    stride = 1
    for size in sizes[axis + 1 :]:
        stride *= size
    return (lax.axis_index("dp") // stride) % sizes[axis]


def gather_level(block, devices, sizes, axis, position):
    size = sizes[axis]
    mine = coordinate(sizes, axis)
    shape = block.shape[:position] + (size,) + block.shape[position:]
    out = jnp.zeros(shape, block.dtype)
    for shift in range(size):
        part = block if shift == 0 else lax.ppermute(block, "dp", cyclic(devices, sizes, axis, shift))
        at = [0] * len(shape)
        at[position] = (mine - shift) % size
        out = lax.dynamic_update_slice(out, jnp.expand_dims(part, position), at)
    return out


def gather_rows(block, devices):
    sizes = levels_of(devices)
    rows, width = block.shape
    cut = (width // 256) * 128
    first, second = block[:, :cut], block[:, cut:]
    first = gather_level(first, devices, sizes, 0, 0)
    second = gather_level(second, devices, sizes, 0, 0)
    first = gather_level(first, devices, sizes, 1, 1)
    second = gather_level(second, devices, sizes, 2, 1)
    first = gather_level(first, devices, sizes, 2, 2)
    second = gather_level(second, devices, sizes, 1, 1)
    both = jnp.concatenate([first, second], axis=-1)
    both = gather_level(both, devices, sizes, 3, 3)
    return both.reshape(devices * rows, width)


def scatter_level(block, devices, sizes, axis, position):
    size = sizes[axis]
    mine = coordinate(sizes, axis)
    total = lax.dynamic_index_in_dim(block, mine, position, keepdims=False)
    for shift in range(1, size):
        part = lax.dynamic_index_in_dim(block, (mine + shift) % size, position, keepdims=False)
        got = lax.ppermute(part.astype(BF16), "dp", cyclic(devices, sizes, axis, shift))
        total = total + got.astype(F32)
    return total


def scatter_rows(grad, devices):
    sizes = levels_of(devices)
    rows, width = grad.shape
    grad = grad.reshape(sizes + (rows // devices, width))
    grad = scatter_level(grad, devices, sizes, 3, 3)
    cut = (width // 256) * 128
    first, second = grad[..., :cut], grad[..., cut:]
    first = scatter_level(first, devices, sizes, 2, 2)
    second = scatter_level(second, devices, sizes, 1, 1)
    first = scatter_level(first, devices, sizes, 1, 1)
    second = scatter_level(second, devices, sizes, 2, 1)
    first = scatter_level(first, devices, sizes, 0, 0)
    second = scatter_level(second, devices, sizes, 0, 0)
    return jnp.concatenate([first, second], axis=-1)


def exchange(slots, experts):
    rows, width = slots.shape
    out = lax.all_to_all(
        slots.reshape(experts, rows // experts, width), "dp", split_axis=0, concat_axis=0, tiled=True
    )
    return out.reshape(rows, width)


def per_device(
    inputs,
    cotangent,
    routes,
    segments,
    qkv_weight,
    query_bias,
    value_bias,
    out_weight,
    out_bias,
    attn_gain,
    attn_shift,
    moe_gain,
    moe_shift,
    router_weight,
    expert_in,
    expert_in_bias,
    expert_out,
    expert_out_bias,
):
    seq_count, tokens, width = inputs.shape
    devices = lax.axis_size("dp")
    experts = router_weight.shape[1]
    capacity = 2 * tokens // devices
    per_chunk = capacity // CHUNKS
    chunk_rows = experts * per_chunk
    wide = width // GROUPS
    rows = qkv_weight.shape[0]
    x = inputs.reshape(tokens, width)
    dy = cotangent.reshape(tokens, width)

    blocks = qkv_weight.reshape(rows, 3, GROUPS, wide).transpose(0, 2, 1, 3)
    blocks = blocks.reshape(rows, GROUPS, 3 * wide).astype(BF16)
    early = jnp.stack([attn_gain, attn_shift, query_bias, value_bias], axis=1).astype(BF16)
    early = jnp.pad(early, ((0, 0), (0, 128 - early.shape[1])))
    late = jnp.concatenate(
        [router_weight, out_bias[:, None], moe_gain[:, None], moe_shift[:, None]], axis=1
    ).astype(BF16)
    late = jnp.pad(late, ((0, 0), (0, -late.shape[1] % 128)))
    full_early = gather_rows(jnp.concatenate([blocks[:, 0], early], axis=1), devices)
    full_late = gather_rows(
        jnp.concatenate([blocks[:, 1], blocks[:, 2], out_weight.astype(BF16), late], axis=1), devices
    )
    weights = (full_early[:, : 3 * wide], full_late[:, : 3 * wide], full_late[:, 3 * wide : 6 * wide])
    proj_out = full_late[:, 6 * wide : 6 * wide + width]
    router = full_late[:, 6 * wide + width :]
    early_rows = full_early[:, 3 * wide : 3 * wide + 8].astype(F32).T
    late_rows = router.astype(F32).T
    vecs = jnp.pad(late_rows[experts : experts + 3], ((0, 5), (0, 0)))
    router_row = lax.dynamic_index_in_dim(late_rows, lax.axis_index("dp"), 0, keepdims=True)

    route = routes.reshape(tokens)
    onehot = route[:, None] == jnp.arange(experts, dtype=jnp.int32)[None, :]
    place = jnp.arange(tokens, dtype=jnp.int32)
    earlier = jnp.dot(
        (place[None, :] < place[:, None]).astype(BF16),
        onehot.astype(BF16),
        preferred_element_type=F32,
    )
    slot = jnp.sum(jnp.where(onehot, earlier, 0.0), axis=1).astype(jnp.int32)
    target = (slot // per_chunk) * chunk_rows + route * per_chunk + slot % per_chunk
    target_row, target_col = target[None, :], target[:, None]

    dys = [exchange(pack(dy, target_row, c * chunk_rows, chunk_rows), experts) for c in range(CHUNKS)]
    w_in = expert_in[0].astype(BF16)
    w_out = expert_out[0].astype(BF16)

    seg_row = segments.reshape(1, tokens)
    seg_col = segments.reshape(tokens, 1)
    scaled, _ = norm_stats(x.astype(F32))
    normed = (scaled * early_rows[0:1] + early_rows[1:2]).astype(BF16)
    qkvs, mixes, lses = [], [], []
    for g in range(GROUPS):
        cols = slice(g * wide, (g + 1) * wide)
        bias = jnp.concatenate(
            [early_rows[2:3, cols], jnp.zeros((1, wide), F32), early_rows[3:4, cols]], axis=1
        )
        qkv, mix, lse = attend(normed, weights[g], bias, seg_col, seg_row)
        qkvs.append(qkv)
        mixes.append(mix)
        lses.append(lse)
    hidden, moe_in = project(x, mixes, proj_out, vecs)

    expert_vecs = jnp.concatenate([expert_out_bias, router_row, jnp.zeros((6, width), F32)], axis=0)
    returned, dmoes, kept = [], [], ()
    dbias_in = dsums = 0.0
    received = [
        exchange(pack(moe_in, target_row, c * chunk_rows, chunk_rows), experts) for c in range(CHUNKS)
    ]
    for c in range(CHUNKS):
        ret, dmoe, *kept, dbias, sums = expert_chunk(
            c, CHUNKS * chunk_rows, received[c], dys[c], w_in, expert_in_bias, w_out, expert_vecs, kept
        )
        dmoes.append(exchange(dmoe, experts))
        returned.append(ret)
        dbias_in = dbias_in + dbias
        dsums = dsums + sums
    act, dpre, arrived, rows_in = kept
    grad_expert_out = dot_tn(act, arrived)
    grad_expert_in = dot_tn(rows_in, dpre)
    returned = [exchange(r, experts) for r in returned]

    dhid, dattn, mid_sums = middle(dmoes, target_col, hidden, dy, vecs)
    grad_out = scatter_rows(dot_tn(jnp.concatenate(mixes, axis=1), dattn), devices)
    dqkvs, qkv_sums, grad_qkv = [], [], []
    for g in range(GROUPS):
        dqkv, col_sums = attend_back(
            qkvs[g],
            mixes[g],
            dattn,
            proj_out[g * wide : (g + 1) * wide],
            lses[g],
            seg_col,
            seg_row,
        )
        dqkvs.append(dqkv)
        qkv_sums.append(col_sums[0:1])
        grad_qkv.append(scatter_rows(dot_tn(normed, dqkv), devices))
    grad_inputs, last_sums = last(dqkvs, weights, x, dhid, early_rows)
    output = finish_output(returned, target_col, route.reshape(tokens, 1), hidden, moe_in, router)

    grad_query = jnp.concatenate([s[:, :wide] for s in qkv_sums], axis=1)
    grad_value = jnp.concatenate([s[:, 2 * wide :] for s in qkv_sums], axis=1)
    small = jnp.concatenate(
        [grad_query, grad_value, mid_sums[0:3], last_sums[0:2], dsums[0:1]], axis=0
    )
    small = small.reshape(8, devices, rows).transpose(1, 0, 2).reshape(devices, 8 * rows)
    small = jnp.pad(small, ((0, 0), (0, -small.shape[1] % 128)))
    small = lax.all_to_all(small, "dp", split_axis=0, concat_axis=0, tiled=True)
    vectors = jnp.sum(small[:, : 7 * rows], axis=0).reshape(7, rows)
    grad_router = small[:, 7 * rows : 8 * rows].T
    grad_qkv = jnp.stack([g.reshape(rows, 3, wide) for g in grad_qkv], axis=2).reshape(rows, 3 * width)
    return (
        output.reshape(seq_count, tokens, width),
        grad_inputs.reshape(seq_count, tokens, width),
        grad_qkv,
        vectors[0],
        vectors[1],
        grad_out,
        vectors[2],
        vectors[5],
        vectors[6],
        vectors[3],
        vectors[4],
        grad_router,
        grad_expert_in[None],
        dbias_in[0:1],
        grad_expert_out[None],
        dsums[1:2],
    )


def solution(mesh):
    placed = (
        P("dp", None, None),
        P("dp", None, None),
        P("dp", None, None),
        P("dp", None),
        P("dp", None),
        P("dp"),
        P("dp"),
        P("dp", None),
        P("dp"),
        P("dp"),
        P("dp"),
        P("dp"),
        P("dp"),
        P("dp", None),
        P("dp", None, None),
        P("dp", None),
        P("dp", None, None),
        P("dp", None),
    )
    return jax.shard_map(
        per_device,
        mesh=mesh,
        in_specs=placed,
        out_specs=(
            P("dp", None, None),
            P("dp", None, None),
            P("dp", None),
            P("dp"),
            P("dp"),
            P("dp", None),
            P("dp"),
            P("dp"),
            P("dp"),
            P("dp"),
            P("dp"),
            P("dp", None),
            P("dp", None, None),
            P("dp", None),
            P("dp", None, None),
            P("dp", None),
        ),
        check_vma=False,
    )
```

```python
import functools

import jax
import jax.numpy as jnp
from jax import lax
from jax.experimental import pallas as pl
from jax.experimental.pallas import tpu as pltpu
from jax.sharding import PartitionSpec as P


HEAD_DIM = 64
PAIR = 2 * HEAD_DIM
GROUPS = 3
QBLOCK = 256
MAX_DOC = 512
CHUNKS = 2
EPSILON = 1e-05
NEG_FILL = -1000000000.0
SQRT_HALF = 0.7071067811865476
INV_ROOT_TAU = 0.3989422804014327
F32 = jnp.float32
BF16 = jnp.bfloat16
VMEM_LIMIT = 56 * 1024 * 1024


def dot(a, b):
    return lax.dot_general(a, b, (((1,), (0,)), ((), ())), preferred_element_type=F32)


def dot_nt(a, b):
    return lax.dot_general(a, b, (((1,), (1,)), ((), ())), preferred_element_type=F32)


def dot_tn(a, b):
    return lax.dot_general(a, b, (((0,), (0,)), ((), ())), preferred_element_type=F32)


def params():
    return pltpu.CompilerParams(vmem_limit_bytes=VMEM_LIMIT)


def whole(shape):
    return pl.BlockSpec(shape, lambda *_: (0,) * len(shape))


def window(index):
    return max(0, index * QBLOCK - MAX_DOC), (index + 1) * QBLOCK


def iota(shape, axis):
    return lax.broadcasted_iota(jnp.int32, shape, axis)


def norm_stats(value):
    mean = jnp.mean(value, axis=1, keepdims=True)
    centred = value - mean
    spread = jnp.mean(centred * centred, axis=1, keepdims=True)
    inverse = lax.rsqrt(spread + EPSILON)
    return centred * inverse, inverse


def norm_back(grad, scaled, inverse, gain):
    inner = grad * gain
    return inverse * (
        inner
        - jnp.mean(inner, axis=1, keepdims=True)
        - scaled * jnp.mean(inner * scaled, axis=1, keepdims=True)
    )


def attend_kernel(x_ref, w_ref, b_ref, sc_ref, sr_ref, qkv_ref, mix_ref, lse_ref):
    tokens = x_ref.shape[0]
    wide = mix_ref.shape[1]
    pairs = wide // PAIR
    packed = dot(x_ref[...], w_ref[...])
    qkv_ref[:, :wide] = (packed[:, :wide] + b_ref[2:3, :]).astype(BF16)
    qkv_ref[:, wide : 2 * wide] = packed[:, wide : 2 * wide].astype(BF16)
    qkv_ref[:, 2 * wide :] = (packed[:, 2 * wide :] + b_ref[3:4, :]).astype(BF16)
    lane = iota((QBLOCK, PAIR), 1)
    for i in range(tokens // QBLOCK):
        lo, hi = window(i)
        r0 = i * QBLOCK
        rows = slice(r0, r0 + QBLOCK)
        allowed = (sc_ref[rows, :] == sr_ref[:, lo:hi]) & (
            iota((QBLOCK, hi - lo), 1) + lo <= iota((QBLOCK, hi - lo), 0) + r0
        )
        total = jnp.zeros((QBLOCK, PAIR), F32)
        for p in range(pairs):
            q = qkv_ref[rows, p * PAIR : (p + 1) * PAIR] * jnp.asarray(HEAD_DIM**-0.5, BF16)
            k = qkv_ref[lo:hi, wide + p * PAIR : wide + (p + 1) * PAIR]
            v = qkv_ref[lo:hi, 2 * wide + p * PAIR : 2 * wide + (p + 1) * PAIR]
            outs = []
            for h in range(2):
                mine = (lane >= HEAD_DIM) if h else (lane < HEAD_DIM)
                qm = jnp.where(mine, q, jnp.zeros((), BF16))
                s = jnp.where(allowed, dot_nt(qm, k), NEG_FILL)
                top = jnp.max(s, axis=1, keepdims=True)
                e = jnp.exp(s - top)
                l = jnp.sum(e, axis=1, keepdims=True)
                outs.append(dot(e.astype(BF16), v) / l)
                total = jnp.where(lane == 2 * p + h, top + jnp.log(l), total)
            mix_ref[rows, p * PAIR : (p + 1) * PAIR] = jnp.where(
                lane < HEAD_DIM, outs[0], outs[1]
            ).astype(BF16)
        lse_ref[:, rows] = jnp.transpose(total)[: lse_ref.shape[0], :]


def attend(group, normed, weight, block, early_rows, seg_col, seg_row):
    tokens, width = normed.shape
    wide = width // GROUPS
    return pl.pallas_call(
        attend_kernel,
        grid=(1,),
        in_specs=[
            whole(normed.shape),
            pl.BlockSpec((width, 3 * wide), lambda i: (0, block)),
            pl.BlockSpec((8, wide), lambda i: (0, group)),
            whole(seg_col.shape),
            whole(seg_row.shape),
        ],
        out_specs=(whole((tokens, 3 * wide)), whole((tokens, wide)), whole((8, tokens))),
        out_shape=(
            jax.ShapeDtypeStruct((tokens, 3 * wide), BF16),
            jax.ShapeDtypeStruct((tokens, wide), BF16),
            jax.ShapeDtypeStruct((8, tokens), F32),
        ),
        compiler_params=params(),
        name="attend",
    )(normed, weight, early_rows, seg_col, seg_row)


def attend_back_kernel(
    qkv_ref, mix_ref, da_ref, wo_ref, lse_ref, sc_ref, sr_ref, out_ref, sum_ref, do_ref, dk_ref, dv_ref
):
    tokens = qkv_ref.shape[0]
    wide = mix_ref.shape[1]
    pairs = wide // PAIR
    do_ref[...] = dot_nt(da_ref[...], wo_ref[...]).astype(BF16)
    scale = jnp.asarray(HEAD_DIM**-0.5, BF16)
    lane = iota((QBLOCK, PAIR), 1)
    head_of = iota((8, wide), 1) // HEAD_DIM
    select = jnp.where(head_of == iota((8, wide), 0), 1.0, 0.0).astype(F32)
    delta = lax.dot_general(
        select,
        do_ref[...].astype(F32) * mix_ref[...].astype(F32),
        (((1,), (1,)), ((), ())),
        precision=lax.Precision.HIGHEST,
        preferred_element_type=F32,
    )
    for p in range(pairs):
        dk_ref[...] = jnp.zeros_like(dk_ref)
        dv_ref[...] = jnp.zeros_like(dv_ref)
        cq = slice(p * PAIR, (p + 1) * PAIR)
        ck = slice(wide + p * PAIR, wide + (p + 1) * PAIR)
        cv = slice(2 * wide + p * PAIR, 2 * wide + (p + 1) * PAIR)
        for i in range(tokens // QBLOCK):
            lo, hi = window(i)
            r0 = i * QBLOCK
            rows = slice(r0, r0 + QBLOCK)
            allowed = (sc_ref[lo:hi, :] == sr_ref[:, rows]) & (
                iota((hi - lo, QBLOCK), 0) + lo <= iota((hi - lo, QBLOCK), 1) + r0
            )
            q = qkv_ref[rows, cq] * scale
            k = qkv_ref[lo:hi, ck]
            v = qkv_ref[lo:hi, cv]
            g = do_ref[rows, cq]
            dq = jnp.zeros((QBLOCK, PAIR), F32)
            for h in range(2):
                mine = (lane >= HEAD_DIM) if h else (lane < HEAD_DIM)
                qm = jnp.where(mine, q, jnp.zeros((), BF16))
                gm = jnp.where(mine, g, jnp.zeros((), BF16))
                head = 2 * p + h
                s = jnp.where(allowed, dot_nt(k, qm), NEG_FILL)
                probs = jnp.exp(s - lse_ref[head : head + 1, rows])
                dv_ref[lo:hi, :] += dot(probs.astype(BF16), gm)
                ds = (probs * (dot_nt(v, gm) - delta[head : head + 1, rows])).astype(BF16)
                dk_ref[lo:hi, :] += dot(ds, qm)
                dq = jnp.where(mine, dot_tn(ds, k), dq)
            out_ref[rows, cq] = (dq * (HEAD_DIM**-0.5)).astype(BF16)
        out_ref[:, ck] = dk_ref[...].astype(BF16)
        out_ref[:, cv] = dv_ref[...].astype(BF16)
    sum_ref[...] = jnp.broadcast_to(
        jnp.sum(out_ref[...].astype(F32), axis=0, keepdims=True), sum_ref.shape
    )


def attend_back(group, qkv, mix, dattn, weight, block, lse, seg_col, seg_row):
    tokens, wide = mix.shape
    width = dattn.shape[1]
    return pl.pallas_call(
        attend_back_kernel,
        grid=(1,),
        in_specs=[
            whole(qkv.shape),
            whole(mix.shape),
            whole(dattn.shape),
            pl.BlockSpec((wide, width), lambda i: (group, block)),
            whole(lse.shape),
            whole(seg_col.shape),
            whole(seg_row.shape),
        ],
        out_specs=(whole((tokens, 3 * wide)), whole((8, 3 * wide))),
        out_shape=(
            jax.ShapeDtypeStruct((tokens, 3 * wide), BF16),
            jax.ShapeDtypeStruct((8, 3 * wide), F32),
        ),
        scratch_shapes=[
            pltpu.VMEM((tokens, wide), BF16),
            pltpu.VMEM((tokens, PAIR), F32),
            pltpu.VMEM((tokens, PAIR), F32),
        ],
        compiler_params=params(),
        name="attend_back",
    )(qkv, mix, dattn, weight, lse, seg_col, seg_row)


def project_kernel(x_ref, m0_ref, m1_ref, m2_ref, wo_ref, vec_ref, hid_ref, moe_ref):
    wide = m0_ref.shape[1]
    hidden = x_ref[...].astype(F32) + vec_ref[0:1, :]
    for g, ref in enumerate((m0_ref, m1_ref, m2_ref)):
        hidden = hidden + dot(ref[...], wo_ref[g * wide : (g + 1) * wide, :])
    hid_ref[...] = hidden
    scaled, _ = norm_stats(hidden)
    moe_ref[...] = (scaled * vec_ref[1:2, :] + vec_ref[2:3, :]).astype(BF16)


def project(x, mixes, weight, block, vecs):
    tokens, width = x.shape
    wide = mixes[0].shape[1]
    row = lambda n: pl.BlockSpec((QBLOCK, n), lambda i: (i, 0))
    return pl.pallas_call(
        project_kernel,
        grid=(tokens // QBLOCK,),
        in_specs=[row(width), row(wide), row(wide), row(wide)]
        + [pl.BlockSpec((width, width), lambda i: (0, block)), whole(vecs.shape)],
        out_specs=(row(width), row(width)),
        out_shape=(
            jax.ShapeDtypeStruct((tokens, width), F32),
            jax.ShapeDtypeStruct((tokens, width), BF16),
        ),
        compiler_params=params(),
        name="project",
    )(x, *mixes, weight, vecs)


def pack_kernel(base, target_ref, rows_ref, out_ref):
    count = out_ref.shape[0]
    start = base + pl.program_id(0) * count
    hot = iota((count, rows_ref.shape[0]), 0) + start == target_ref[...]
    out_ref[...] = dot(jnp.where(hot, 1.0, 0.0).astype(BF16), rows_ref[...]).astype(BF16)


def pack(rows, target_row, chunk, count):
    tokens, width = rows.shape
    return pl.pallas_call(
        functools.partial(pack_kernel, chunk * count),
        grid=(count // 512,),
        in_specs=[whole((1, tokens)), whole(rows.shape)],
        out_specs=pl.BlockSpec((512, width), lambda i: (i, 0)),
        out_shape=jax.ShapeDtypeStruct((count, width), BF16),
        compiler_params=params(),
        name="pack",
    )(target_row, rows)


def unpack_rows(target, refs):
    base = 0
    picked = None
    for ref in refs:
        count = ref.shape[0]
        hot = iota((target.shape[0], count), 1) + base == target
        part = dot(jnp.where(hot, 1.0, 0.0).astype(BF16), ref[...])
        picked = part if picked is None else picked + part
        base += count
    return picked


def middle_kernel(*refs):
    slots = refs[:CHUNKS]
    tgt_ref, hid_ref, dy_ref, vec_ref, dhid_ref, da_ref, sum_ref = refs[CHUNKS:]
    dmoe = unpack_rows(tgt_ref[...], slots)
    scaled, inverse = norm_stats(hid_ref[...])
    dhid = dy_ref[...].astype(F32) + norm_back(dmoe, scaled, inverse, vec_ref[1:2, :])
    dhid_ref[...] = dhid
    low = dhid.astype(BF16)
    da_ref[...] = low

    @pl.when(pl.program_id(0) == 0)
    def _():
        sum_ref[...] = jnp.zeros_like(sum_ref)

    sum_ref[0:1, :] += jnp.sum(low.astype(F32), axis=0, keepdims=True)
    sum_ref[1:2, :] += jnp.sum(dmoe * scaled, axis=0, keepdims=True)
    sum_ref[2:3, :] += jnp.sum(dmoe, axis=0, keepdims=True)


def middle(slots, target_col, hidden, dy, vecs):
    tokens, width = hidden.shape
    row = lambda n: pl.BlockSpec((QBLOCK, n), lambda i: (i, 0))
    return pl.pallas_call(
        middle_kernel,
        grid=(tokens // QBLOCK,),
        in_specs=[whole(s.shape) for s in slots] + [row(1), row(width), row(width), whole(vecs.shape)],
        out_specs=(row(width), row(width), whole((8, width))),
        out_shape=(
            jax.ShapeDtypeStruct((tokens, width), F32),
            jax.ShapeDtypeStruct((tokens, width), BF16),
            jax.ShapeDtypeStruct((8, width), F32),
        ),
        compiler_params=params(),
        name="middle",
    )(*slots, target_col, hidden, dy, vecs)


def output_kernel(*refs):
    slots = refs[:CHUNKS]
    tgt_ref, route_ref, hid_ref, moe_ref, router_ref, out_ref = refs[CHUNKS:]
    logits = dot(moe_ref[...], router_ref[...])
    chosen = jnp.sum(
        jnp.where(iota(logits.shape, 1) == route_ref[...], logits, 0.0), axis=1, keepdims=True
    )
    gate = jax.nn.sigmoid(chosen)
    out_ref[...] = (hid_ref[...] + gate * unpack_rows(tgt_ref[...], slots)).astype(BF16)


def finish_output(slots, target_col, route_col, hidden, moe_in, weight, at, count):
    tokens, width = hidden.shape
    row = lambda n: pl.BlockSpec((QBLOCK, n), lambda i: (i, 0))
    return pl.pallas_call(
        output_kernel,
        grid=(tokens // QBLOCK,),
        in_specs=[whole(s.shape) for s in slots]
        + [row(1), row(1), row(width), row(width)]
        + [pl.BlockSpec((width, count), lambda i: (0, at // count))],
        out_specs=row(width),
        out_shape=jax.ShapeDtypeStruct((tokens, width), BF16),
        compiler_params=params(),
        name="finish_output",
    )(*slots, target_col, route_col, hidden, moe_in, weight)


def last_kernel(d0_ref, d1_ref, d2_ref, w0_ref, w1_ref, w2_ref, x_ref, dhid_ref, vec_ref, out_ref, sum_ref):
    grad = dot_nt(d0_ref[...], w0_ref[...])
    grad = grad + dot_nt(d1_ref[...], w1_ref[...])
    grad = grad + dot_nt(d2_ref[...], w2_ref[...])
    scaled, inverse = norm_stats(x_ref[...].astype(F32))
    out_ref[...] = dhid_ref[...] + norm_back(grad, scaled, inverse, vec_ref[0:1, :])

    @pl.when(pl.program_id(0) == 0)
    def _():
        sum_ref[...] = jnp.zeros_like(sum_ref)

    sum_ref[0:1, :] += jnp.sum(grad * scaled, axis=0, keepdims=True)
    sum_ref[1:2, :] += jnp.sum(grad, axis=0, keepdims=True)


def last(dqkvs, weights, blocks, x, dhid, vecs):
    tokens, width = x.shape
    row = lambda n: pl.BlockSpec((QBLOCK, n), lambda i: (i, 0))
    return pl.pallas_call(
        last_kernel,
        grid=(tokens // QBLOCK,),
        in_specs=[row(d.shape[1]) for d in dqkvs]
        + [pl.BlockSpec((width, width), functools.partial(lambda b, i: (0, b), b)) for b in blocks]
        + [row(width), row(width), whole(vecs.shape)],
        out_specs=(row(width), whole((8, width))),
        out_shape=(
            jax.ShapeDtypeStruct((tokens, width), F32),
            jax.ShapeDtypeStruct((8, width), F32),
        ),
        compiler_params=params(),
        name="last",
    )(*dqkvs, *weights, x, dhid, vecs)


def expert_kernel(aliased, *refs):
    x_ref, dy_ref, wi_ref, bi_ref, wo_ref, vec_ref = refs[:6]
    refs = refs[6 + aliased :]
    ret_ref, dmoe_ref, act_ref, dpre_ref, arr_ref, xall_ref, gbi_ref, sum_ref = refs[:8]
    accr_ref, accg_ref = refs[8:]
    step = pl.program_id(0)

    def gate_of():
        x = x_ref[...].astype(F32)
        return jax.nn.sigmoid(jnp.sum(x * vec_ref[1:2, :], axis=1, keepdims=True))

    @pl.when(step == 0)
    def _():
        arr_ref[...] = (dy_ref[...].astype(F32) * gate_of()).astype(BF16)
        xall_ref[...] = x_ref[...]
        accr_ref[...] = jnp.broadcast_to(vec_ref[0:1, :], accr_ref.shape)
        accg_ref[...] = jnp.zeros_like(accg_ref)

    pre = dot(x_ref[...], wi_ref[...]) + bi_ref[...]
    dact = dot_nt(arr_ref[...], wo_ref[...])
    phi = 0.5 * (1.0 + lax.erf(pre * SQRT_HALF))
    act = (pre * phi).astype(BF16)
    act_ref[...] = act
    accr_ref[...] += dot(act, wo_ref[...])
    slope = phi + pre * jnp.exp(-0.5 * pre * pre) * INV_ROOT_TAU
    dpre = (dact * slope).astype(BF16)
    dpre_ref[...] = dpre
    accg_ref[...] += dot_nt(dpre, wi_ref[...])
    gbi_ref[...] = jnp.broadcast_to(
        jnp.sum(dpre.astype(F32), axis=0, keepdims=True), gbi_ref.shape
    )

    @pl.when(step == pl.num_programs(0) - 1)
    def _():
        gate = gate_of()
        ret = accr_ref[...].astype(BF16)
        ret_ref[...] = ret
        dgate = jnp.sum(dy_ref[...].astype(F32) * ret.astype(F32), axis=1, keepdims=True)
        dlogit = (dgate * gate * (1.0 - gate)).astype(BF16).astype(F32)
        dmoe_ref[...] = (
            accg_ref[...].astype(BF16).astype(F32) + dlogit * vec_ref[1:2, :]
        ).astype(BF16)
        sum_ref[...] = jnp.zeros_like(sum_ref)
        sum_ref[0:1, :] = jnp.sum(x_ref[...].astype(F32) * dlogit, axis=0, keepdims=True)
        sum_ref[1:2, :] = jnp.sum(arr_ref[...].astype(F32), axis=0, keepdims=True)


def expert_chunk(chunk, total, x, dy, w_in, b_in, w_out, vecs, kept):
    rows, width = x.shape
    hidden = w_in.shape[1]
    block = 512
    aliased = len(kept)
    any_spec = pl.BlockSpec(memory_space=pl.ANY)
    return pl.pallas_call(
        functools.partial(expert_kernel, aliased),
        grid=(hidden // block,),
        in_specs=[
            whole(x.shape),
            whole(dy.shape),
            pl.BlockSpec((width, block), lambda f: (0, f)),
            pl.BlockSpec((1, block), lambda f: (0, f)),
            pl.BlockSpec((block, width), lambda f: (f, 0)),
            whole(vecs.shape),
        ]
        + [any_spec] * aliased,
        out_specs=(
            whole((rows, width)),
            whole((rows, width)),
            pl.BlockSpec((rows, block), lambda f: (chunk, f)),
            pl.BlockSpec((rows, block), lambda f: (chunk, f)),
            pl.BlockSpec((rows, width), lambda f: (chunk, 0)),
            pl.BlockSpec((rows, width), lambda f: (chunk, 0)),
            pl.BlockSpec((8, block), lambda f: (0, f)),
            whole((8, width)),
        ),
        out_shape=(
            jax.ShapeDtypeStruct((rows, width), BF16),
            jax.ShapeDtypeStruct((rows, width), BF16),
            jax.ShapeDtypeStruct((total, hidden), BF16),
            jax.ShapeDtypeStruct((total, hidden), BF16),
            jax.ShapeDtypeStruct((total, width), BF16),
            jax.ShapeDtypeStruct((total, width), BF16),
            jax.ShapeDtypeStruct((8, hidden), F32),
            jax.ShapeDtypeStruct((8, width), F32),
        ),
        scratch_shapes=[pltpu.VMEM((rows, width), F32), pltpu.VMEM((rows, width), F32)],
        input_output_aliases={6 + i: 2 + i for i in range(aliased)},
        compiler_params=params(),
        name="expert",
    )(x, dy, w_in, b_in, w_out, vecs, *kept)


def levels_of(devices):
    side = int(round((devices // 8) ** 0.5))
    return (devices // (2 * side * side), side, side, 2)


def cyclic(devices, sizes, axis, shift):
    stride = 1
    for size in sizes[axis + 1 :]:
        stride *= size
    pairs = []
    for i in range(devices):
        at = (i // stride) % sizes[axis]
        pairs.append((i, i + ((at + shift) % sizes[axis] - at) * stride))
    return pairs


def coordinate(sizes, axis):
    stride = 1
    for size in sizes[axis + 1 :]:
        stride *= size
    return lax.rem(lax.div(lax.axis_index("dp"), stride), sizes[axis])


def shifted(block, devices, sizes, axis):
    parts = [block]
    for shift in range(1, sizes[axis]):
        parts.append(lax.ppermute(block, "dp", cyclic(devices, sizes, axis, shift)))
    return parts


def in_order(parts, mine, position):
    size = len(parts)
    slots = []
    for j in range(size):
        back = lax.rem(mine + (size - j), size)
        slot = parts[0]
        for shift in range(1, size):
            slot = jnp.where(back == shift, parts[shift], slot)
        slots.append(slot)
    return jnp.stack(slots, axis=position)


def gather_level(block, devices, sizes, axis, position):
    return in_order(shifted(block, devices, sizes, axis), coordinate(sizes, axis), position)


def gather_rows(block, devices):
    sizes = levels_of(devices)
    rows, width = block.shape
    cut = (width // 256) * 128
    block = gather_level(block, devices, sizes, 0, 0)
    first, second = block[..., :cut], block[..., cut:]
    first = gather_level(first, devices, sizes, 1, 1)
    second = gather_level(second, devices, sizes, 2, 1)
    first = gather_level(first, devices, sizes, 2, 2)
    second = gather_level(second, devices, sizes, 1, 1)
    both = jnp.concatenate([first, second], axis=-1)
    both = gather_level(both, devices, sizes, 3, 3)
    return both.reshape(devices * rows, width)


def scatter_level(blocks, devices, sizes, axis, position):
    size = sizes[axis]
    mine = coordinate(sizes, axis)
    totals = [lax.dynamic_index_in_dim(block, mine, position, keepdims=False) for block in blocks]
    for shift in range(1, size):
        other = lax.rem(mine + shift, size)
        parts = [
            lax.dynamic_index_in_dim(block, other, position, keepdims=False).astype(BF16) for block in blocks
        ]
        part = jnp.concatenate(parts, axis=-1) if len(parts) > 1 else parts[0]
        got = lax.ppermute(part, "dp", cyclic(devices, sizes, axis, shift))
        base = 0
        for n, total in enumerate(totals):
            width = total.shape[-1]
            totals[n] = total + got[..., base : base + width].astype(F32)
            base += width
    return totals


def scatter_rows(first, second, devices):
    sizes = levels_of(devices)
    count = len(first)
    both = [g.reshape(sizes + (g.shape[0] // devices, g.shape[1])) for g in first + second]
    both = scatter_level(both, devices, sizes, 3, 3)
    first, second = both[:count], both[count:]
    first = scatter_level(first, devices, sizes, 2, 2)
    if second:
        second = scatter_level(second, devices, sizes, 1, 1)
    first = scatter_level(first, devices, sizes, 1, 1)
    if second:
        second = scatter_level(second, devices, sizes, 2, 1)
    return scatter_level(first + second, devices, sizes, 0, 0)


def exchange(slots, experts):
    rows, width = slots.shape
    out = lax.all_to_all(slots.reshape(experts, rows // experts, width), "dp", split_axis=0, concat_axis=0, tiled=True)
    return out.reshape(rows, width)


def per_device(
    inputs,
    cotangent,
    routes,
    segments,
    qkv_weight,
    query_bias,
    value_bias,
    out_weight,
    out_bias,
    attn_gain,
    attn_shift,
    moe_gain,
    moe_shift,
    router_weight,
    expert_in,
    expert_in_bias,
    expert_out,
    expert_out_bias,
):
    seq_count, tokens, width = inputs.shape
    devices = lax.axis_size("dp")
    experts = router_weight.shape[1]
    capacity = 2 * tokens // devices
    per_chunk = capacity // CHUNKS
    chunk_rows = experts * per_chunk
    wide = width // GROUPS
    rows = qkv_weight.shape[0]
    x = inputs.reshape(tokens, width)
    dy = cotangent.reshape(tokens, width)

    blocks = qkv_weight.reshape(rows, 3, GROUPS, wide).transpose(0, 2, 1, 3)
    blocks = blocks.reshape(rows, GROUPS, 3 * wide).astype(BF16)
    early = jnp.stack([attn_gain, attn_shift, query_bias, value_bias], axis=1).astype(BF16)
    early = jnp.pad(early, ((0, 0), (0, 128 - early.shape[1])))
    late = jnp.concatenate(
        [router_weight, out_bias[:, None], moe_gain[:, None], moe_shift[:, None]], axis=1
    ).astype(BF16)
    late = jnp.pad(late, ((0, 0), (0, -late.shape[1] % 128)))
    full_early = gather_rows(jnp.concatenate([blocks[:, 0], early], axis=1), devices)
    full_late = gather_rows(
        jnp.concatenate([blocks[:, 1], blocks[:, 2], out_weight.astype(BF16), late], axis=1), devices
    )
    weights = (full_early, full_late, full_late)
    places = (0, 0, 1)
    out_place = 2
    router_at, router_wide = 6 * wide + width, late.shape[1]
    early_rows = full_early[:, 3 * wide : 3 * wide + 8].astype(F32).T
    late_rows = full_late[:, router_at:].astype(F32).T
    vecs = jnp.pad(late_rows[experts : experts + 3], ((0, 5), (0, 0)))
    router_row = lax.dynamic_index_in_dim(late_rows, lax.axis_index("dp"), 0, keepdims=True)

    route = routes.reshape(tokens)
    onehot = route[:, None] == jnp.arange(experts, dtype=jnp.int32)[None, :]
    place = jnp.arange(tokens, dtype=jnp.int32)
    earlier = jnp.dot(
        (place[None, :] < place[:, None]).astype(BF16),
        onehot.astype(BF16),
        preferred_element_type=F32,
    )
    slot = jnp.sum(jnp.where(onehot, earlier, 0.0), axis=1).astype(jnp.int32)
    target = (slot // per_chunk) * chunk_rows + route * per_chunk + slot % per_chunk
    target_row, target_col = target[None, :], target[:, None]

    dys = [exchange(pack(dy, target_row, c, chunk_rows), experts) for c in range(CHUNKS)]
    w_in = expert_in[0].astype(BF16)
    w_out = expert_out[0].astype(BF16)

    seg_row = segments.reshape(1, tokens)
    seg_col = segments.reshape(tokens, 1)
    scaled, _ = norm_stats(x.astype(F32))
    normed = (scaled * early_rows[0:1] + early_rows[1:2]).astype(BF16)
    qkvs, mixes, lses = [], [], []
    for g in range(GROUPS):
        qkv, mix, lse = attend(g, normed, weights[g], places[g], early_rows, seg_col, seg_row)
        qkvs.append(qkv)
        mixes.append(mix)
        lses.append(lse)
    hidden, moe_in = project(x, mixes, full_late, out_place, vecs)

    expert_vecs = jnp.concatenate([expert_out_bias, router_row, jnp.zeros((6, width), F32)], axis=0)
    returned, dmoes, kept = [], [], ()
    dbias_in = dsums = 0.0
    received = [exchange(pack(moe_in, target_row, c, chunk_rows), experts) for c in range(CHUNKS)]
    for c in range(CHUNKS):
        ret, dmoe, *kept, dbias, sums = expert_chunk(
            c, CHUNKS * chunk_rows, received[c], dys[c], w_in, expert_in_bias, w_out, expert_vecs, kept
        )
        dmoes.append(exchange(dmoe, experts))
        returned.append(ret)
        dbias_in = dbias_in + dbias
        dsums = dsums + sums
    act, dpre, arrived, rows_in = kept
    grad_expert_out = dot_tn(act, arrived)
    grad_expert_in = dot_tn(rows_in, dpre)
    returned = [exchange(r, experts) for r in returned]

    dhid, dattn, mid_sums = middle(dmoes, target_col, hidden, dy, vecs)
    part_out = dot_tn(jnp.concatenate(mixes, axis=1), dattn)
    dqkvs, qkv_sums, parts = [None] * GROUPS, [None] * GROUPS, [None] * GROUPS
    for g in reversed(range(GROUPS)):
        dqkvs[g], col_sums = attend_back(g, qkvs[g], mixes[g], dattn, full_late, out_place, lses[g], seg_col, seg_row)
        qkv_sums[g] = col_sums[0:1]
        parts[g] = dot_tn(normed, dqkvs[g])
    grad_out, *upper = scatter_rows([part_out], parts[1:], devices)
    grad_qkv = scatter_rows(parts[:1], [], devices) + upper
    grad_inputs, last_sums = last(dqkvs, weights, places, x, dhid, early_rows)
    output = finish_output(
        returned, target_col, route.reshape(tokens, 1), hidden, moe_in, full_late, router_at, router_wide
    )

    grad_query = jnp.concatenate([s[:, :wide] for s in qkv_sums], axis=1)
    grad_value = jnp.concatenate([s[:, 2 * wide :] for s in qkv_sums], axis=1)
    small = jnp.concatenate(
        [grad_query, grad_value, mid_sums[0:3], last_sums[0:2], dsums[0:1]], axis=0
    )
    small = small.reshape(8, devices, rows).transpose(1, 0, 2).reshape(devices, 8 * rows)
    small = jnp.pad(small, ((0, 0), (0, -small.shape[1] % 128)))
    small = lax.all_to_all(small, "dp", split_axis=0, concat_axis=0, tiled=True)
    vectors = jnp.sum(small[:, : 7 * rows], axis=0).reshape(7, rows)
    grad_router = small[:, 7 * rows : 8 * rows].T
    grad_qkv = jnp.stack([g.reshape(rows, 3, wide) for g in grad_qkv], axis=2).reshape(rows, 3 * width)
    return (
        output.reshape(seq_count, tokens, width),
        grad_inputs.reshape(seq_count, tokens, width),
        grad_qkv,
        vectors[0],
        vectors[1],
        grad_out,
        vectors[2],
        vectors[5],
        vectors[6],
        vectors[3],
        vectors[4],
        grad_router,
        grad_expert_in[None],
        dbias_in[0:1],
        grad_expert_out[None],
        dsums[1:2],
    )


def solution(mesh):
    placed = (
        P("dp", None, None),
        P("dp", None, None),
        P("dp", None, None),
        P("dp", None),
        P("dp", None),
        P("dp"),
        P("dp"),
        P("dp", None),
        P("dp"),
        P("dp"),
        P("dp"),
        P("dp"),
        P("dp"),
        P("dp", None),
        P("dp", None, None),
        P("dp", None),
        P("dp", None, None),
        P("dp", None),
    )
    return jax.shard_map(
        per_device,
        mesh=mesh,
        in_specs=placed,
        out_specs=(
            P("dp", None, None),
            P("dp", None, None),
            P("dp", None),
            P("dp"),
            P("dp"),
            P("dp", None),
            P("dp"),
            P("dp"),
            P("dp"),
            P("dp"),
            P("dp"),
            P("dp", None),
            P("dp", None, None),
            P("dp", None),
            P("dp", None, None),
            P("dp", None),
        ),
        check_vma=False,
    )
```

```python
import functools

import jax
import jax.numpy as jnp
from jax import lax
from jax.experimental import pallas as pl
from jax.experimental.pallas import tpu as pltpu
from jax.sharding import PartitionSpec as P


HEAD_DIM = 64
PAIR = 2 * HEAD_DIM
GROUPS = 3
QBLOCK = 256
MAX_DOC = 512
CHUNKS = 2
EPSILON = 1e-05
NEG_FILL = -1000000000.0
SQRT_HALF = 0.7071067811865476
INV_ROOT_TAU = 0.3989422804014327
F32 = jnp.float32
BF16 = jnp.bfloat16
VMEM_LIMIT = 56 * 1024 * 1024


def dot(a, b):
    return lax.dot_general(a, b, (((1,), (0,)), ((), ())), preferred_element_type=F32)


def dot_nt(a, b):
    return lax.dot_general(a, b, (((1,), (1,)), ((), ())), preferred_element_type=F32)


def dot_tn(a, b):
    return lax.dot_general(a, b, (((0,), (0,)), ((), ())), preferred_element_type=F32)


def params():
    return pltpu.CompilerParams(vmem_limit_bytes=VMEM_LIMIT)


def whole(shape):
    return pl.BlockSpec(shape, lambda *_: (0,) * len(shape))


def window(index):
    return max(0, index * QBLOCK - MAX_DOC), (index + 1) * QBLOCK


def iota(shape, axis):
    return lax.broadcasted_iota(jnp.int32, shape, axis)


def norm_stats(value):
    mean = jnp.mean(value, axis=1, keepdims=True)
    centred = value - mean
    spread = jnp.mean(centred * centred, axis=1, keepdims=True)
    inverse = lax.rsqrt(spread + EPSILON)
    return centred * inverse, inverse


def norm_back(grad, scaled, inverse, gain):
    inner = grad * gain
    return inverse * (
        inner
        - jnp.mean(inner, axis=1, keepdims=True)
        - scaled * jnp.mean(inner * scaled, axis=1, keepdims=True)
    )


def attend_kernel(x_ref, w_ref, b_ref, sc_ref, sr_ref, qkv_ref, mix_ref, lse_ref):
    tokens = x_ref.shape[0]
    wide = mix_ref.shape[1]
    pairs = wide // PAIR
    packed = dot(x_ref[...], w_ref[...])
    qkv_ref[:, :wide] = (packed[:, :wide] + b_ref[2:3, :]).astype(BF16)
    qkv_ref[:, wide : 2 * wide] = packed[:, wide : 2 * wide].astype(BF16)
    qkv_ref[:, 2 * wide :] = (packed[:, 2 * wide :] + b_ref[3:4, :]).astype(BF16)
    lane = iota((QBLOCK, PAIR), 1)
    for i in range(tokens // QBLOCK):
        lo, hi = window(i)
        r0 = i * QBLOCK
        rows = slice(r0, r0 + QBLOCK)
        allowed = (sc_ref[rows, :] == sr_ref[:, lo:hi]) & (
            iota((QBLOCK, hi - lo), 1) + lo <= iota((QBLOCK, hi - lo), 0) + r0
        )
        total = jnp.zeros((QBLOCK, PAIR), F32)
        for p in range(pairs):
            q = qkv_ref[rows, p * PAIR : (p + 1) * PAIR] * jnp.asarray(HEAD_DIM**-0.5, BF16)
            k = qkv_ref[lo:hi, wide + p * PAIR : wide + (p + 1) * PAIR]
            v = qkv_ref[lo:hi, 2 * wide + p * PAIR : 2 * wide + (p + 1) * PAIR]
            outs = []
            for h in range(2):
                mine = (lane >= HEAD_DIM) if h else (lane < HEAD_DIM)
                qm = jnp.where(mine, q, jnp.zeros((), BF16))
                s = jnp.where(allowed, dot_nt(qm, k), NEG_FILL)
                top = jnp.max(s, axis=1, keepdims=True)
                e = jnp.exp(s - top)
                l = jnp.sum(e, axis=1, keepdims=True)
                outs.append(dot(e.astype(BF16), v) / l)
                total = jnp.where(lane == 2 * p + h, top + jnp.log(l), total)
            mix_ref[rows, p * PAIR : (p + 1) * PAIR] = jnp.where(
                lane < HEAD_DIM, outs[0], outs[1]
            ).astype(BF16)
        lse_ref[:, rows] = jnp.transpose(total)[: lse_ref.shape[0], :]


def attend(group, normed, weight, block, early_rows, seg_col, seg_row):
    tokens, width = normed.shape
    wide = width // GROUPS
    return pl.pallas_call(
        attend_kernel,
        grid=(1,),
        in_specs=[
            whole(normed.shape),
            pl.BlockSpec((width, 3 * wide), lambda i: (0, block)),
            pl.BlockSpec((8, wide), lambda i: (0, group)),
            whole(seg_col.shape),
            whole(seg_row.shape),
        ],
        out_specs=(whole((tokens, 3 * wide)), whole((tokens, wide)), whole((8, tokens))),
        out_shape=(
            jax.ShapeDtypeStruct((tokens, 3 * wide), BF16),
            jax.ShapeDtypeStruct((tokens, wide), BF16),
            jax.ShapeDtypeStruct((8, tokens), F32),
        ),
        compiler_params=params(),
        name="attend",
    )(normed, weight, early_rows, seg_col, seg_row)


def halves(grad, part_ref, own_ref):
    half = part_ref.shape[0]
    part_ref[...] = grad[:half].astype(BF16)
    own_ref[...] = grad[half:]


def outer_kernel(turned_ref, grad_ref, part_ref, own_ref):
    halves(dot(turned_ref[...], grad_ref[...]), part_ref, own_ref)


def outer(turned, grad, blocks):
    rows, _ = turned.shape
    width = grad.shape[1]
    return pl.pallas_call(
        outer_kernel,
        grid=(1,),
        in_specs=[whole(turned.shape), whole(grad.shape)],
        out_specs=(
            pl.BlockSpec((rows // 2, width), lambda i: (0, blocks - 1)),
            whole((rows // 2, width)),
        ),
        out_shape=(
            jax.ShapeDtypeStruct((rows // 2, blocks * width), BF16),
            jax.ShapeDtypeStruct((rows // 2, width), F32),
        ),
        compiler_params=params(),
        name="outer",
    )(turned, grad)


def attend_back_kernel(
    qkv_ref,
    mix_ref,
    da_ref,
    wo_ref,
    lse_ref,
    sc_ref,
    sr_ref,
    turned_ref,
    _,
    out_ref,
    sum_ref,
    part_ref,
    own_ref,
    do_ref,
    dk_ref,
    dv_ref,
):
    tokens = qkv_ref.shape[0]
    wide = mix_ref.shape[1]
    pairs = wide // PAIR
    do_ref[...] = dot_nt(da_ref[...], wo_ref[...]).astype(BF16)
    scale = jnp.asarray(HEAD_DIM**-0.5, BF16)
    lane = iota((QBLOCK, PAIR), 1)
    head_of = iota((8, wide), 1) // HEAD_DIM
    select = jnp.where(head_of == iota((8, wide), 0), 1.0, 0.0).astype(F32)
    delta = lax.dot_general(
        select,
        do_ref[...].astype(F32) * mix_ref[...].astype(F32),
        (((1,), (1,)), ((), ())),
        precision=lax.Precision.HIGHEST,
        preferred_element_type=F32,
    )
    for p in range(pairs):
        dk_ref[...] = jnp.zeros_like(dk_ref)
        dv_ref[...] = jnp.zeros_like(dv_ref)
        cq = slice(p * PAIR, (p + 1) * PAIR)
        ck = slice(wide + p * PAIR, wide + (p + 1) * PAIR)
        cv = slice(2 * wide + p * PAIR, 2 * wide + (p + 1) * PAIR)
        for i in range(tokens // QBLOCK):
            lo, hi = window(i)
            r0 = i * QBLOCK
            rows = slice(r0, r0 + QBLOCK)
            allowed = (sc_ref[lo:hi, :] == sr_ref[:, rows]) & (
                iota((hi - lo, QBLOCK), 0) + lo <= iota((hi - lo, QBLOCK), 1) + r0
            )
            q = qkv_ref[rows, cq] * scale
            k = qkv_ref[lo:hi, ck]
            v = qkv_ref[lo:hi, cv]
            g = do_ref[rows, cq]
            dq = jnp.zeros((QBLOCK, PAIR), F32)
            for h in range(2):
                mine = (lane >= HEAD_DIM) if h else (lane < HEAD_DIM)
                qm = jnp.where(mine, q, jnp.zeros((), BF16))
                gm = jnp.where(mine, g, jnp.zeros((), BF16))
                head = 2 * p + h
                s = jnp.where(allowed, dot_nt(k, qm), NEG_FILL)
                probs = jnp.exp(s - lse_ref[head : head + 1, rows])
                dv_ref[lo:hi, :] += dot(probs.astype(BF16), gm)
                ds = (probs * (dot_nt(v, gm) - delta[head : head + 1, rows])).astype(BF16)
                dk_ref[lo:hi, :] += dot(ds, qm)
                dq = jnp.where(mine, dot_tn(ds, k), dq)
            out_ref[rows, cq] = (dq * (HEAD_DIM**-0.5)).astype(BF16)
        out_ref[:, ck] = dk_ref[...].astype(BF16)
        out_ref[:, cv] = dv_ref[...].astype(BF16)
    sum_ref[...] = jnp.broadcast_to(
        jnp.sum(out_ref[...].astype(F32), axis=0, keepdims=True), sum_ref.shape
    )
    halves(dot(turned_ref[...], out_ref[...]), part_ref, own_ref)


def attend_back(group, qkv, mix, dattn, weight, block, lse, seg_col, seg_row, turned, parts):
    tokens, wide = mix.shape
    width = dattn.shape[1]
    return pl.pallas_call(
        attend_back_kernel,
        grid=(1,),
        in_specs=[
            whole(qkv.shape),
            whole(mix.shape),
            whole(dattn.shape),
            pl.BlockSpec((wide, width), lambda i: (group, block)),
            whole(lse.shape),
            whole(seg_col.shape),
            whole(seg_row.shape),
            whole(turned.shape),
            pl.BlockSpec(memory_space=pl.ANY),
        ],
        out_specs=(
            whole((tokens, 3 * wide)),
            whole((8, 3 * wide)),
            pl.BlockSpec((width // 2, 3 * wide), lambda i: (0, group)),
            whole((width // 2, 3 * wide)),
        ),
        input_output_aliases={8: 2},
        out_shape=(
            jax.ShapeDtypeStruct((tokens, 3 * wide), BF16),
            jax.ShapeDtypeStruct((8, 3 * wide), F32),
            jax.ShapeDtypeStruct(parts.shape, BF16),
            jax.ShapeDtypeStruct((width // 2, 3 * wide), F32),
        ),
        scratch_shapes=[
            pltpu.VMEM((tokens, wide), BF16),
            pltpu.VMEM((tokens, PAIR), F32),
            pltpu.VMEM((tokens, PAIR), F32),
        ],
        compiler_params=params(),
        name="attend_back",
    )(qkv, mix, dattn, weight, lse, seg_col, seg_row, turned, parts)


def project_kernel(x_ref, m0_ref, m1_ref, m2_ref, wo_ref, vec_ref, hid_ref, moe_ref):
    wide = m0_ref.shape[1]
    hidden = x_ref[...].astype(F32) + vec_ref[0:1, :]
    for g, ref in enumerate((m0_ref, m1_ref, m2_ref)):
        hidden = hidden + dot(ref[...], wo_ref[g * wide : (g + 1) * wide, :])
    hid_ref[...] = hidden
    scaled, _ = norm_stats(hidden)
    moe_ref[...] = (scaled * vec_ref[1:2, :] + vec_ref[2:3, :]).astype(BF16)


def project(x, mixes, weight, block, vecs):
    tokens, width = x.shape
    wide = mixes[0].shape[1]
    row = lambda n: pl.BlockSpec((QBLOCK, n), lambda i: (i, 0))
    return pl.pallas_call(
        project_kernel,
        grid=(tokens // QBLOCK,),
        in_specs=[row(width), row(wide), row(wide), row(wide)]
        + [pl.BlockSpec((width, width), lambda i: (0, block)), whole(vecs.shape)],
        out_specs=(row(width), row(width)),
        out_shape=(
            jax.ShapeDtypeStruct((tokens, width), F32),
            jax.ShapeDtypeStruct((tokens, width), BF16),
        ),
        compiler_params=params(),
        name="project",
    )(x, *mixes, weight, vecs)


def pack_kernel(base, target_ref, rows_ref, *refs):
    out_ref = refs[-1]
    count = out_ref.shape[0]
    start = base + pl.program_id(0) * count
    hot = iota((count, rows_ref.shape[0]), 0) + start == target_ref[...]
    out_ref[...] = dot(jnp.where(hot, 1.0, 0.0).astype(BF16), rows_ref[...]).astype(BF16)


def pack(rows, target_row, base, count, total, kept=()):
    tokens, width = rows.shape
    block = 512
    first = base % total // block
    return pl.pallas_call(
        functools.partial(pack_kernel, base),
        grid=(count // block,),
        in_specs=[whole((1, tokens)), whole(rows.shape)]
        + [pl.BlockSpec(memory_space=pl.ANY)] * len(kept),
        out_specs=pl.BlockSpec((block, width), lambda i: (first + i, 0)),
        out_shape=jax.ShapeDtypeStruct((total, width), BF16),
        input_output_aliases={2: 0} if kept else {},
        compiler_params=params(),
        name="pack",
    )(target_row, rows, *kept)


def unpack_rows(target, refs):
    base = 0
    picked = None
    for ref in refs:
        count = ref.shape[0]
        hot = iota((target.shape[0], count), 1) + base == target
        part = dot(jnp.where(hot, 1.0, 0.0).astype(BF16), ref[...])
        picked = part if picked is None else picked + part
        base += count
    return picked


def middle_kernel(*refs):
    slots = refs[:CHUNKS]
    tgt_ref, hid_ref, dy_ref, vec_ref, dhid_ref, da_ref, sum_ref = refs[CHUNKS:]
    dmoe = unpack_rows(tgt_ref[...], slots)
    scaled, inverse = norm_stats(hid_ref[...])
    dhid = dy_ref[...].astype(F32) + norm_back(dmoe, scaled, inverse, vec_ref[1:2, :])
    dhid_ref[...] = dhid
    low = dhid.astype(BF16)
    da_ref[...] = low

    @pl.when(pl.program_id(0) == 0)
    def _():
        sum_ref[...] = jnp.zeros_like(sum_ref)

    sum_ref[0:1, :] += jnp.sum(low.astype(F32), axis=0, keepdims=True)
    sum_ref[1:2, :] += jnp.sum(dmoe * scaled, axis=0, keepdims=True)
    sum_ref[2:3, :] += jnp.sum(dmoe, axis=0, keepdims=True)


def middle(slots, target_col, hidden, dy, vecs):
    tokens, width = hidden.shape
    row = lambda n: pl.BlockSpec((QBLOCK, n), lambda i: (i, 0))
    return pl.pallas_call(
        middle_kernel,
        grid=(tokens // QBLOCK,),
        in_specs=[whole(s.shape) for s in slots] + [row(1), row(width), row(width), whole(vecs.shape)],
        out_specs=(row(width), row(width), whole((8, width))),
        out_shape=(
            jax.ShapeDtypeStruct((tokens, width), F32),
            jax.ShapeDtypeStruct((tokens, width), BF16),
            jax.ShapeDtypeStruct((8, width), F32),
        ),
        compiler_params=params(),
        name="middle",
    )(*slots, target_col, hidden, dy, vecs)


def output_kernel(slots_ref, tgt_ref, route_ref, hid_ref, moe_ref, router_ref, out_ref):
    logits = dot(moe_ref[...], router_ref[...])
    chosen = jnp.sum(
        jnp.where(iota(logits.shape, 1) == route_ref[...], logits, 0.0), axis=1, keepdims=True
    )
    gate = jax.nn.sigmoid(chosen)
    out_ref[...] = (hid_ref[...] + gate * unpack_rows(tgt_ref[...], [slots_ref])).astype(BF16)


def finish_output(slots, target_col, route_col, hidden, moe_in, weight, at, count):
    tokens, width = hidden.shape
    row = lambda n: pl.BlockSpec((QBLOCK, n), lambda i: (i, 0))
    return pl.pallas_call(
        output_kernel,
        grid=(tokens // QBLOCK,),
        in_specs=[whole(slots.shape), row(1), row(1), row(width), row(width)]
        + [pl.BlockSpec((width, count), lambda i: (0, at // count))],
        out_specs=row(width),
        out_shape=jax.ShapeDtypeStruct((tokens, width), BF16),
        compiler_params=params(),
        name="finish_output",
    )(slots, target_col, route_col, hidden, moe_in, weight)


def last_kernel(d0_ref, d1_ref, d2_ref, w0_ref, w1_ref, w2_ref, x_ref, dhid_ref, vec_ref, out_ref, sum_ref):
    grad = dot_nt(d0_ref[...], w0_ref[...])
    grad = grad + dot_nt(d1_ref[...], w1_ref[...])
    grad = grad + dot_nt(d2_ref[...], w2_ref[...])
    scaled, inverse = norm_stats(x_ref[...].astype(F32))
    out_ref[...] = dhid_ref[...] + norm_back(grad, scaled, inverse, vec_ref[0:1, :])

    @pl.when(pl.program_id(0) == 0)
    def _():
        sum_ref[...] = jnp.zeros_like(sum_ref)

    sum_ref[0:1, :] += jnp.sum(grad * scaled, axis=0, keepdims=True)
    sum_ref[1:2, :] += jnp.sum(grad, axis=0, keepdims=True)


def last(dqkvs, weights, blocks, x, dhid, vecs):
    tokens, width = x.shape
    row = lambda n: pl.BlockSpec((QBLOCK, n), lambda i: (i, 0))
    return pl.pallas_call(
        last_kernel,
        grid=(tokens // QBLOCK,),
        in_specs=[row(d.shape[1]) for d in dqkvs]
        + [pl.BlockSpec((width, width), functools.partial(lambda b, i: (0, b), b)) for b in blocks]
        + [row(width), row(width), whole(vecs.shape)],
        out_specs=(row(width), whole((8, width))),
        out_shape=(
            jax.ShapeDtypeStruct((tokens, width), F32),
            jax.ShapeDtypeStruct((8, width), F32),
        ),
        compiler_params=params(),
        name="last",
    )(*dqkvs, *weights, x, dhid, vecs)


def expert_kernel(aliased, *refs):
    x_ref, dy_ref, wi_ref, bi_ref, wo_ref, vec_ref = refs[:6]
    refs = refs[6 + aliased :]
    ret_ref, dmoe_ref, act_ref, dpre_ref, arr_ref, xall_ref, gbi_ref, sum_ref = refs[:8]
    accr_ref, accg_ref = refs[8:]
    step = pl.program_id(0)

    def gate_of():
        x = x_ref[...].astype(F32)
        return jax.nn.sigmoid(jnp.sum(x * vec_ref[1:2, :], axis=1, keepdims=True))

    @pl.when(step == 0)
    def _():
        arr_ref[...] = (dy_ref[...].astype(F32) * gate_of()).astype(BF16)
        xall_ref[...] = x_ref[...]
        accr_ref[...] = jnp.broadcast_to(vec_ref[0:1, :], accr_ref.shape)
        accg_ref[...] = jnp.zeros_like(accg_ref)

    pre = dot(x_ref[...], wi_ref[...]) + bi_ref[...]
    dact = dot_nt(arr_ref[...], wo_ref[...])
    phi = 0.5 * (1.0 + lax.erf(pre * SQRT_HALF))
    act = (pre * phi).astype(BF16)
    act_ref[...] = act
    accr_ref[...] += dot(act, wo_ref[...])
    slope = phi + pre * jnp.exp(-0.5 * pre * pre) * INV_ROOT_TAU
    dpre = (dact * slope).astype(BF16)
    dpre_ref[...] = dpre
    accg_ref[...] += dot_nt(dpre, wi_ref[...])
    gbi_ref[...] = jnp.broadcast_to(
        jnp.sum(dpre.astype(F32), axis=0, keepdims=True), gbi_ref.shape
    )

    @pl.when(step == pl.num_programs(0) - 1)
    def _():
        gate = gate_of()
        ret = accr_ref[...].astype(BF16)
        ret_ref[...] = ret
        dgate = jnp.sum(dy_ref[...].astype(F32) * ret.astype(F32), axis=1, keepdims=True)
        dlogit = (dgate * gate * (1.0 - gate)).astype(BF16).astype(F32)
        dmoe_ref[...] = (
            accg_ref[...].astype(BF16).astype(F32) + dlogit * vec_ref[1:2, :]
        ).astype(BF16)
        sum_ref[...] = jnp.zeros_like(sum_ref)
        sum_ref[0:1, :] = jnp.sum(x_ref[...].astype(F32) * dlogit, axis=0, keepdims=True)
        sum_ref[1:2, :] = jnp.sum(arr_ref[...].astype(F32), axis=0, keepdims=True)


def expert_chunk(chunk, total, x, dy, w_in, b_in, w_out, vecs, kept):
    rows, width = x.shape
    hidden = w_in.shape[1]
    block = 512
    aliased = len(kept)
    any_spec = pl.BlockSpec(memory_space=pl.ANY)
    return pl.pallas_call(
        functools.partial(expert_kernel, aliased),
        grid=(hidden // block,),
        in_specs=[
            whole(x.shape),
            whole(dy.shape),
            pl.BlockSpec((width, block), lambda f: (0, f)),
            pl.BlockSpec((1, block), lambda f: (0, f)),
            pl.BlockSpec((block, width), lambda f: (f, 0)),
            whole(vecs.shape),
        ]
        + [any_spec] * aliased,
        out_specs=(
            whole((rows, width)),
            whole((rows, width)),
            pl.BlockSpec((rows, block), lambda f: (chunk, f)),
            pl.BlockSpec((rows, block), lambda f: (chunk, f)),
            pl.BlockSpec((rows, width), lambda f: (chunk, 0)),
            pl.BlockSpec((rows, width), lambda f: (chunk, 0)),
            pl.BlockSpec((8, block), lambda f: (0, f)),
            whole((8, width)),
        ),
        out_shape=(
            jax.ShapeDtypeStruct((rows, width), BF16),
            jax.ShapeDtypeStruct((rows, width), BF16),
            jax.ShapeDtypeStruct((total, hidden), BF16),
            jax.ShapeDtypeStruct((total, hidden), BF16),
            jax.ShapeDtypeStruct((total, width), BF16),
            jax.ShapeDtypeStruct((total, width), BF16),
            jax.ShapeDtypeStruct((8, hidden), F32),
            jax.ShapeDtypeStruct((8, width), F32),
        ),
        scratch_shapes=[pltpu.VMEM((rows, width), F32), pltpu.VMEM((rows, width), F32)],
        input_output_aliases={6 + i: 2 + i for i in range(aliased)},
        compiler_params=params(),
        name="expert",
    )(x, dy, w_in, b_in, w_out, vecs, *kept)


def levels_of(devices):
    side = int(round((devices // 8) ** 0.5))
    return (devices // (2 * side * side), side, side, 2)


def cyclic(devices, sizes, axis, shift):
    stride = 1
    for size in sizes[axis + 1 :]:
        stride *= size
    pairs = []
    for i in range(devices):
        at = (i // stride) % sizes[axis]
        pairs.append((i, i + ((at + shift) % sizes[axis] - at) * stride))
    return pairs


def coordinate(sizes, axis):
    stride = 1
    for size in sizes[axis + 1 :]:
        stride *= size
    return lax.rem(lax.div(lax.axis_index("dp"), stride), sizes[axis])


def shifted(block, devices, sizes, axis):
    parts = [block]
    for shift in range(1, sizes[axis]):
        parts.append(lax.ppermute(block, "dp", cyclic(devices, sizes, axis, shift)))
    return parts


def in_order(parts, mine, position):
    size = len(parts)
    slots = []
    for j in range(size):
        back = lax.rem(mine + (size - j), size)
        slot = parts[0]
        for shift in range(1, size):
            slot = jnp.where(back == shift, parts[shift], slot)
        slots.append(slot)
    return jnp.stack(slots, axis=position)


def gather_level(block, devices, sizes, axis, position):
    return in_order(shifted(block, devices, sizes, axis), coordinate(sizes, axis), position)


def gather_rows(block, devices):
    sizes = levels_of(devices)
    rows, width = block.shape
    cut = (width // 256) * 128
    block = gather_level(block, devices, sizes, 0, 0)
    first, second = block[..., :cut], block[..., cut:]
    first = gather_level(first, devices, sizes, 1, 1)
    second = gather_level(second, devices, sizes, 2, 1)
    first = gather_level(first, devices, sizes, 2, 2)
    second = gather_level(second, devices, sizes, 1, 1)
    both = jnp.concatenate([first, second], axis=-1)
    both = gather_level(both, devices, sizes, 3, 3)
    return both.reshape(devices * rows, width)


def scatter_level(blocks, devices, sizes, axis, position):
    size = sizes[axis]
    mine = coordinate(sizes, axis)
    totals = [lax.dynamic_index_in_dim(block, mine, position, keepdims=False) for block in blocks]
    for shift in range(1, size):
        other = lax.rem(mine + shift, size)
        parts = [
            lax.dynamic_index_in_dim(block, other, position, keepdims=False).astype(BF16) for block in blocks
        ]
        part = jnp.concatenate(parts, axis=-1) if len(parts) > 1 else parts[0]
        got = lax.ppermute(part, "dp", cyclic(devices, sizes, axis, shift))
        base = 0
        for n, total in enumerate(totals):
            width = total.shape[-1]
            totals[n] = total + got[..., base : base + width].astype(F32)
            base += width
    return totals


def scatter_rows(parts, owns, split, devices):
    sizes = levels_of(devices)
    got = lax.ppermute(parts, "dp", cyclic(devices, sizes, 3, 1))
    width = owns[0].shape[1]
    shape = sizes[:3] + (owns[0].shape[0] * 2 // devices, width)
    both = [
        (own + got[:, n * width : (n + 1) * width].astype(F32)).reshape(shape) for n, own in enumerate(owns)
    ]
    first, second = both[:split], both[split:]
    first = scatter_level(first, devices, sizes, 2, 2)
    second = scatter_level(second, devices, sizes, 1, 1)
    first = scatter_level(first, devices, sizes, 1, 1)
    second = scatter_level(second, devices, sizes, 2, 1)
    return scatter_level(first + second, devices, sizes, 0, 0)


def other_first(rows, devices):
    place = coordinate(levels_of(devices), 3)
    split = rows.reshape(devices // 2, 2, rows.shape[0] // devices, rows.shape[1])
    pick = lambda index: lax.dynamic_index_in_dim(split, index, 1, keepdims=False)
    return jnp.concatenate([pick(1 - place), pick(place)], axis=0).reshape(rows.shape)


def exchange(slots, experts):
    rows, width = slots.shape
    out = lax.all_to_all(slots.reshape(experts, rows // experts, width), "dp", split_axis=0, concat_axis=0, tiled=True)
    return out.reshape(rows, width)


def per_device(
    inputs,
    cotangent,
    routes,
    segments,
    qkv_weight,
    query_bias,
    value_bias,
    out_weight,
    out_bias,
    attn_gain,
    attn_shift,
    moe_gain,
    moe_shift,
    router_weight,
    expert_in,
    expert_in_bias,
    expert_out,
    expert_out_bias,
):
    seq_count, tokens, width = inputs.shape
    devices = lax.axis_size("dp")
    experts = router_weight.shape[1]
    capacity = 2 * tokens // devices
    per_chunk = capacity // CHUNKS
    chunk_rows = experts * per_chunk
    wide = width // GROUPS
    rows = qkv_weight.shape[0]
    x = inputs.reshape(tokens, width)
    dy = cotangent.reshape(tokens, width)

    blocks = qkv_weight.reshape(rows, 3, GROUPS, wide).transpose(0, 2, 1, 3)
    blocks = blocks.reshape(rows, GROUPS, 3 * wide).astype(BF16)
    early = jnp.stack([attn_gain, attn_shift, query_bias, value_bias], axis=1).astype(BF16)
    early = jnp.pad(early, ((0, 0), (0, 128 - early.shape[1])))
    late = jnp.concatenate(
        [router_weight, out_bias[:, None], moe_gain[:, None], moe_shift[:, None]], axis=1
    ).astype(BF16)
    late = jnp.pad(late, ((0, 0), (0, -late.shape[1] % 128)))
    full_early = gather_rows(jnp.concatenate([blocks[:, 0], early], axis=1), devices)
    full_late = gather_rows(
        jnp.concatenate([blocks[:, 1], blocks[:, 2], out_weight.astype(BF16), late], axis=1), devices
    )
    weights = (full_early, full_late, full_late)
    places = (0, 0, 1)
    out_place = 2
    router_at, router_wide = 6 * wide + width, late.shape[1]
    early_rows = full_early[:, 3 * wide : 3 * wide + 8].astype(F32).T
    late_rows = full_late[:, router_at:].astype(F32).T
    vecs = jnp.pad(late_rows[experts : experts + 3], ((0, 5), (0, 0)))
    router_row = lax.dynamic_index_in_dim(late_rows, lax.axis_index("dp"), 0, keepdims=True)

    route = routes.reshape(tokens)
    onehot = route[:, None] == jnp.arange(experts, dtype=jnp.int32)[None, :]
    place = jnp.arange(tokens, dtype=jnp.int32)
    earlier = jnp.dot(
        (place[None, :] < place[:, None]).astype(BF16),
        onehot.astype(BF16),
        preferred_element_type=F32,
    )
    slot = jnp.sum(jnp.where(onehot, earlier, 0.0), axis=1).astype(jnp.int32)

    def places_of(route, slot):
        chunk = sum(jnp.where(slot >= n * per_chunk, 1, 0) for n in range(1, CHUNKS))
        return chunk * (chunk_rows - per_chunk) + route * per_chunk + slot, route * capacity + slot

    target_row, entire_row = places_of(route[None, :], slot[None, :])
    route_col = route[:, None]
    target_col, entire_col = places_of(route_col, slot[:, None])

    slots = CHUNKS * chunk_rows
    dy_slots = ()
    for c in range(CHUNKS):
        dy_slots = (
            pack(dy, entire_row, c * chunk_rows, chunk_rows, slots, dy_slots),
        )
    dy_slots = exchange(dy_slots[0], experts).reshape(experts, CHUNKS, per_chunk, width)
    dys = [dy_slots[:, c].reshape(chunk_rows, width) for c in range(CHUNKS)]
    w_in = expert_in[0].astype(BF16)
    w_out = expert_out[0].astype(BF16)

    seg_row = segments.reshape(1, tokens)
    seg_col = segments.reshape(tokens, 1)
    scaled, _ = norm_stats(x.astype(F32))
    normed = (scaled * early_rows[0:1] + early_rows[1:2]).astype(BF16)
    qkvs, mixes, lses = [], [], []
    for g in range(GROUPS):
        qkv, mix, lse = attend(g, normed, weights[g], places[g], early_rows, seg_col, seg_row)
        qkvs.append(qkv)
        mixes.append(mix)
        lses.append(lse)
    hidden, moe_in = project(x, mixes, full_late, out_place, vecs)

    expert_vecs = jnp.concatenate([expert_out_bias, router_row, jnp.zeros((6, width), F32)], axis=0)
    returned, dmoes, kept = [], [], ()
    dbias_in = dsums = 0.0
    received = [
        exchange(pack(moe_in, target_row, c * chunk_rows, chunk_rows, chunk_rows), experts)
        for c in range(CHUNKS)
    ]
    mix_t = other_first(jnp.concatenate(mixes, axis=1).T, devices)
    normed_t = other_first(normed.T, devices)
    received[0], target_col, entire_col, route_col, mix_t, normed_t = lax.optimization_barrier(
        (received[0], target_col, entire_col, route_col, mix_t, normed_t)
    )
    for c in range(CHUNKS):
        ret, dmoe, *kept, dbias, sums = expert_chunk(
            c, CHUNKS * chunk_rows, received[c], dys[c], w_in, expert_in_bias, w_out, expert_vecs, kept
        )
        dmoes.append(exchange(dmoe, experts))
        returned.append(ret)
        dbias_in = dbias_in + dbias
        dsums = dsums + sums
    act, dpre, arrived, rows_in = kept
    grad_expert_out = dot_tn(act, arrived)
    grad_expert_in = dot_tn(rows_in, dpre)
    returned = jnp.stack([r.reshape(experts, per_chunk, width) for r in returned], axis=1)
    returned = exchange(returned.reshape(slots, width), experts)

    dhid, dattn, mid_sums = middle(dmoes, target_col, hidden, dy, vecs)
    parts, own_out = outer(mix_t, dattn, GROUPS + 1)
    dqkvs, qkv_sums, owns = [], [], []
    for g in range(GROUPS):
        dqkv, col_sums, parts, own = attend_back(
            g, qkvs[g], mixes[g], dattn, full_late, out_place, lses[g], seg_col, seg_row, normed_t, parts
        )
        dqkvs.append(dqkv)
        qkv_sums.append(col_sums[0:1])
        owns.append(own)
    *grad_qkv, grad_out = scatter_rows(parts, owns + [own_out], 2, devices)
    grad_inputs, last_sums = last(dqkvs, weights, places, x, dhid, early_rows)
    output = finish_output(
        returned, entire_col, route_col, hidden, moe_in, full_late, router_at, router_wide
    )

    grad_query = jnp.concatenate([s[:, :wide] for s in qkv_sums], axis=1)
    grad_value = jnp.concatenate([s[:, 2 * wide :] for s in qkv_sums], axis=1)
    small = jnp.concatenate(
        [grad_query, grad_value, mid_sums[0:3], last_sums[0:2], dsums[0:1]], axis=0
    )
    small = small.reshape(8, devices, rows).transpose(1, 0, 2).reshape(devices, 8 * rows)
    small = jnp.pad(small, ((0, 0), (0, -small.shape[1] % 128)))
    small = lax.all_to_all(small, "dp", split_axis=0, concat_axis=0, tiled=True)
    vectors = jnp.sum(small[:, : 7 * rows], axis=0).reshape(7, rows)
    grad_router = small[:, 7 * rows : 8 * rows].T
    grad_qkv = jnp.stack([g.reshape(rows, 3, wide) for g in grad_qkv], axis=2).reshape(rows, 3 * width)
    return (
        output.reshape(seq_count, tokens, width),
        grad_inputs.reshape(seq_count, tokens, width),
        grad_qkv,
        vectors[0],
        vectors[1],
        grad_out,
        vectors[2],
        vectors[5],
        vectors[6],
        vectors[3],
        vectors[4],
        grad_router,
        grad_expert_in[None],
        dbias_in[0:1],
        grad_expert_out[None],
        dsums[1:2],
    )


def solution(mesh):
    placed = (
        P("dp", None, None),
        P("dp", None, None),
        P("dp", None, None),
        P("dp", None),
        P("dp", None),
        P("dp"),
        P("dp"),
        P("dp", None),
        P("dp"),
        P("dp"),
        P("dp"),
        P("dp"),
        P("dp"),
        P("dp", None),
        P("dp", None, None),
        P("dp", None),
        P("dp", None, None),
        P("dp", None),
    )
    return jax.shard_map(
        per_device,
        mesh=mesh,
        in_specs=placed,
        out_specs=(
            P("dp", None, None),
            P("dp", None, None),
            P("dp", None),
            P("dp"),
            P("dp"),
            P("dp", None),
            P("dp"),
            P("dp"),
            P("dp"),
            P("dp"),
            P("dp"),
            P("dp", None),
            P("dp", None, None),
            P("dp", None),
            P("dp", None, None),
            P("dp", None),
        ),
        check_vma=False,
    )
```

```python
import functools

import jax
import jax.numpy as jnp
from jax import lax
from jax.experimental import pallas as pl
from jax.experimental.pallas import tpu as pltpu
from jax.sharding import PartitionSpec as P


HEAD_DIM = 64
PAIR = 2 * HEAD_DIM
GROUPS = 3
QBLOCK = 256
MAX_DOC = 512
CHUNKS = 2
EPSILON = 1e-05
NEG_FILL = -1000000000.0
SQRT_HALF = 0.7071067811865476
INV_ROOT_TAU = 0.3989422804014327
F32 = jnp.float32
BF16 = jnp.bfloat16
VMEM_LIMIT = 56 * 1024 * 1024


def dot(a, b):
    return lax.dot_general(a, b, (((1,), (0,)), ((), ())), preferred_element_type=F32)


def dot_nt(a, b):
    return lax.dot_general(a, b, (((1,), (1,)), ((), ())), preferred_element_type=F32)


def dot_tn(a, b):
    return lax.dot_general(a, b, (((0,), (0,)), ((), ())), preferred_element_type=F32)


def params():
    return pltpu.CompilerParams(vmem_limit_bytes=VMEM_LIMIT)


def whole(shape):
    return pl.BlockSpec(shape, lambda *_: (0,) * len(shape))


def window(index):
    return max(0, index * QBLOCK - MAX_DOC), (index + 1) * QBLOCK


def iota(shape, axis):
    return lax.broadcasted_iota(jnp.int32, shape, axis)


def norm_stats(value):
    mean = jnp.mean(value, axis=1, keepdims=True)
    centred = value - mean
    spread = jnp.mean(centred * centred, axis=1, keepdims=True)
    inverse = lax.rsqrt(spread + EPSILON)
    return centred * inverse, inverse


def norm_back(grad, scaled, inverse, gain):
    inner = grad * gain
    return inverse * (
        inner
        - jnp.mean(inner, axis=1, keepdims=True)
        - scaled * jnp.mean(inner * scaled, axis=1, keepdims=True)
    )


def attend_kernel(x_ref, w_ref, b_ref, sc_ref, sr_ref, qkv_ref, mix_ref, lse_ref):
    tokens = x_ref.shape[0]
    wide = mix_ref.shape[1]
    pairs = wide // PAIR
    packed = dot(x_ref[...], w_ref[...])
    qkv_ref[:, :wide] = (packed[:, :wide] + b_ref[2:3, :]).astype(BF16)
    qkv_ref[:, wide : 2 * wide] = packed[:, wide : 2 * wide].astype(BF16)
    qkv_ref[:, 2 * wide :] = (packed[:, 2 * wide :] + b_ref[3:4, :]).astype(BF16)
    lane = iota((QBLOCK, PAIR), 1)
    for i in range(tokens // QBLOCK):
        lo, hi = window(i)
        r0 = i * QBLOCK
        rows = slice(r0, r0 + QBLOCK)
        allowed = (sc_ref[rows, :] == sr_ref[:, lo:hi]) & (
            iota((QBLOCK, hi - lo), 1) + lo <= iota((QBLOCK, hi - lo), 0) + r0
        )
        total = jnp.zeros((QBLOCK, PAIR), F32)
        for p in range(pairs):
            q = qkv_ref[rows, p * PAIR : (p + 1) * PAIR] * jnp.asarray(HEAD_DIM**-0.5, BF16)
            k = qkv_ref[lo:hi, wide + p * PAIR : wide + (p + 1) * PAIR]
            v = qkv_ref[lo:hi, 2 * wide + p * PAIR : 2 * wide + (p + 1) * PAIR]
            outs = []
            for h in range(2):
                mine = (lane >= HEAD_DIM) if h else (lane < HEAD_DIM)
                qm = jnp.where(mine, q, jnp.zeros((), BF16))
                s = jnp.where(allowed, dot_nt(qm, k), NEG_FILL)
                top = jnp.max(s, axis=1, keepdims=True)
                e = jnp.exp(s - top)
                l = jnp.sum(e, axis=1, keepdims=True)
                outs.append(dot(e.astype(BF16), v) / l)
                total = jnp.where(lane == 2 * p + h, top + jnp.log(l), total)
            mix_ref[rows, p * PAIR : (p + 1) * PAIR] = jnp.where(
                lane < HEAD_DIM, outs[0], outs[1]
            ).astype(BF16)
        lse_ref[:, rows] = jnp.transpose(total)[: lse_ref.shape[0], :]


def attend(normed, weights, early_rows, seg_col, seg_row):
    tokens, width = normed.shape
    wide = width // GROUPS
    column = lambda rows, n: pl.BlockSpec((rows, n), lambda g: (0, g))
    return pl.pallas_call(
        attend_kernel,
        grid=(GROUPS,),
        in_specs=[
            whole(normed.shape),
            column(width, 3 * wide),
            column(8, wide),
            whole(seg_col.shape),
            whole(seg_row.shape),
        ],
        out_specs=(
            column(tokens, 3 * wide),
            column(tokens, wide),
            pl.BlockSpec((8, tokens), lambda g: (g, 0)),
        ),
        out_shape=(
            jax.ShapeDtypeStruct((tokens, 3 * width), BF16),
            jax.ShapeDtypeStruct((tokens, width), BF16),
            jax.ShapeDtypeStruct((8 * GROUPS, tokens), F32),
        ),
        compiler_params=params(),
        name="attend",
    )(normed, weights, early_rows, seg_col, seg_row)


def halves(grad, part_ref, own_ref):
    half = part_ref.shape[0]
    part_ref[...] = grad[:half].astype(BF16)
    own_ref[...] = grad[half:]


def behind_kernel(
    qkv_ref,
    mix_ref,
    da_ref,
    wo_ref,
    lse_ref,
    sc_ref,
    sr_ref,
    turned_ref,
    mix_t_ref,
    w_ref,
    vec_ref,
    x_hbm,
    dhid_hbm,
    sum_ref,
    part_ref,
    own_ref,
    grad_ref,
    last_ref,
    out_ref,
    do_ref,
    dk_ref,
    dv_ref,
    acc_ref,
    x_ref,
    dhid_ref,
    sems,
):
    step = pl.program_id(0)
    copies = (
        pltpu.make_async_copy(x_hbm, x_ref, sems.at[0]),
        pltpu.make_async_copy(dhid_hbm, dhid_ref, sems.at[1]),
    )

    @pl.when(step == 0)
    def _():
        for copy in copies:
            copy.start()
        halves(dot(mix_t_ref[...], da_ref[...]), part_ref, own_ref)
        acc_ref[...] = jnp.zeros_like(acc_ref)

    @pl.when(step > 0)
    def _():
        attend_back(
            qkv_ref, mix_ref, da_ref, wo_ref, lse_ref, sc_ref, sr_ref, out_ref, sum_ref, do_ref, dk_ref, dv_ref
        )
        halves(dot(turned_ref[...], out_ref[...]), part_ref, own_ref)
        acc_ref[...] += dot_nt(out_ref[...], w_ref[...])

    @pl.when(step == pl.num_programs(0) - 1)
    def _():
        for copy in copies:
            copy.wait()
        last_ref[...] = jnp.zeros_like(last_ref)
        for r in range(0, x_ref.shape[0], QBLOCK):
            rows = slice(r, r + QBLOCK)
            grad = acc_ref[rows, :]
            scaled, inverse = norm_stats(x_ref[rows, :].astype(F32))
            grad_ref[rows, :] = dhid_ref[rows, :] + norm_back(grad, scaled, inverse, vec_ref[0:1, :])
            last_ref[0:1, :] += jnp.sum(grad * scaled, axis=0, keepdims=True)
            last_ref[1:2, :] += jnp.sum(grad, axis=0, keepdims=True)


def attend_back(
    qkv_ref, mix_ref, da_ref, wo_ref, lse_ref, sc_ref, sr_ref, out_ref, sum_ref, do_ref, dk_ref, dv_ref
):
    tokens = qkv_ref.shape[0]
    wide = mix_ref.shape[1]
    pairs = wide // PAIR
    do_ref[...] = dot_nt(da_ref[...], wo_ref[...]).astype(BF16)
    scale = jnp.asarray(HEAD_DIM**-0.5, BF16)
    lane = iota((QBLOCK, PAIR), 1)
    head_of = iota((8, wide), 1) // HEAD_DIM
    select = jnp.where(head_of == iota((8, wide), 0), 1.0, 0.0).astype(F32)
    delta = lax.dot_general(
        select,
        do_ref[...].astype(F32) * mix_ref[...].astype(F32),
        (((1,), (1,)), ((), ())),
        precision=lax.Precision.HIGHEST,
        preferred_element_type=F32,
    )
    for p in range(pairs):
        dk_ref[...] = jnp.zeros_like(dk_ref)
        dv_ref[...] = jnp.zeros_like(dv_ref)
        cq = slice(p * PAIR, (p + 1) * PAIR)
        ck = slice(wide + p * PAIR, wide + (p + 1) * PAIR)
        cv = slice(2 * wide + p * PAIR, 2 * wide + (p + 1) * PAIR)
        for i in range(tokens // QBLOCK):
            lo, hi = window(i)
            r0 = i * QBLOCK
            rows = slice(r0, r0 + QBLOCK)
            allowed = (sc_ref[lo:hi, :] == sr_ref[:, rows]) & (
                iota((hi - lo, QBLOCK), 0) + lo <= iota((hi - lo, QBLOCK), 1) + r0
            )
            q = qkv_ref[rows, cq] * scale
            k = qkv_ref[lo:hi, ck]
            v = qkv_ref[lo:hi, cv]
            g = do_ref[rows, cq]
            dq = jnp.zeros((QBLOCK, PAIR), F32)
            for h in range(2):
                mine = (lane >= HEAD_DIM) if h else (lane < HEAD_DIM)
                qm = jnp.where(mine, q, jnp.zeros((), BF16))
                gm = jnp.where(mine, g, jnp.zeros((), BF16))
                head = 2 * p + h
                s = jnp.where(allowed, dot_nt(k, qm), NEG_FILL)
                probs = jnp.exp(s - lse_ref[head : head + 1, rows])
                dv_ref[lo:hi, :] += dot(probs.astype(BF16), gm)
                ds = (probs * (dot_nt(v, gm) - delta[head : head + 1, rows])).astype(BF16)
                dk_ref[lo:hi, :] += dot(ds, qm)
                dq = jnp.where(mine, dot_tn(ds, k), dq)
            out_ref[rows, cq] = (dq * (HEAD_DIM**-0.5)).astype(BF16)
        out_ref[:, ck] = dk_ref[...].astype(BF16)
        out_ref[:, cv] = dv_ref[...].astype(BF16)
    sum_ref[...] = jnp.broadcast_to(
        jnp.sum(out_ref[...].astype(F32), axis=0, keepdims=True), sum_ref.shape
    )


def behind(qkv, mix, dattn, weights, lse, seg_col, seg_row, turned, mix_t, vecs, x, dhid):
    tokens, width = mix.shape
    wide = width // GROUPS
    steps = GROUPS + 1
    group = lambda i: jnp.maximum(i - 1, 0)
    column = lambda rows, n: pl.BlockSpec((rows, n), lambda i: (0, group(i)))
    piece = pl.BlockSpec((width // 2, width), lambda i: (0, lax.rem(i + GROUPS, steps)))
    hbm = pl.BlockSpec(memory_space=pl.ANY)
    return pl.pallas_call(
        behind_kernel,
        grid=(steps,),
        in_specs=[
            column(tokens, 3 * wide),
            column(tokens, wide),
            whole(dattn.shape),
            pl.BlockSpec((wide, width), lambda i: (group(i), GROUPS)),
            pl.BlockSpec((8, tokens), lambda i: (group(i), 0)),
            whole(seg_col.shape),
            whole(seg_row.shape),
            whole(turned.shape),
            whole(mix_t.shape),
            column(width, 3 * wide),
            whole(vecs.shape),
            hbm,
            hbm,
        ],
        out_specs=(column(8, 3 * wide), piece, piece, whole((tokens, width)), whole((8, width))),
        out_shape=(
            jax.ShapeDtypeStruct((8, 3 * width), F32),
            jax.ShapeDtypeStruct((width // 2, steps * width), BF16),
            jax.ShapeDtypeStruct((width // 2, steps * width), F32),
            jax.ShapeDtypeStruct((tokens, width), F32),
            jax.ShapeDtypeStruct((8, width), F32),
        ),
        scratch_shapes=[
            pltpu.VMEM((tokens, 3 * wide), BF16),
            pltpu.VMEM((tokens, wide), BF16),
            pltpu.VMEM((tokens, PAIR), F32),
            pltpu.VMEM((tokens, PAIR), F32),
            pltpu.VMEM((tokens, width), F32),
            pltpu.VMEM((tokens, width), x.dtype),
            pltpu.VMEM((tokens, width), F32),
            pltpu.SemaphoreType.DMA((2,)),
        ],
        compiler_params=params(),
        name="behind",
    )(qkv, mix, dattn, weights, lse, seg_col, seg_row, turned, mix_t, weights, vecs, x, dhid)


def project_kernel(x_ref, mix_ref, wo_ref, vec_ref, hid_ref, moe_ref):
    hidden = x_ref[...].astype(F32) + vec_ref[0:1, :]
    hidden = hidden + dot(mix_ref[...], wo_ref[...])
    hid_ref[...] = hidden
    scaled, _ = norm_stats(hidden)
    moe_ref[...] = (scaled * vec_ref[1:2, :] + vec_ref[2:3, :]).astype(BF16)


def project(x, mix, weights, vecs):
    tokens, width = x.shape
    row = lambda n: pl.BlockSpec((QBLOCK, n), lambda i: (i, 0))
    return pl.pallas_call(
        project_kernel,
        grid=(tokens // QBLOCK,),
        in_specs=[
            row(width),
            row(width),
            pl.BlockSpec((width, width), lambda i: (0, GROUPS)),
            whole(vecs.shape),
        ],
        out_specs=(row(width), row(width)),
        out_shape=(
            jax.ShapeDtypeStruct((tokens, width), F32),
            jax.ShapeDtypeStruct((tokens, width), BF16),
        ),
        compiler_params=params(),
        name="project",
    )(x, mix, weights, vecs)


def pack_kernel(base, target_ref, rows_ref, *refs):
    out_ref = refs[-1]
    count = out_ref.shape[0]
    start = base + pl.program_id(0) * count
    hot = iota((count, rows_ref.shape[0]), 0) + start == target_ref[...]
    out_ref[...] = dot(jnp.where(hot, 1.0, 0.0).astype(BF16), rows_ref[...]).astype(BF16)


def pack(rows, target_row, base, count, total, kept=()):
    tokens, width = rows.shape
    block = 512
    first = base % total // block
    return pl.pallas_call(
        functools.partial(pack_kernel, base),
        grid=(count // block,),
        in_specs=[whole((1, tokens)), whole(rows.shape)]
        + [pl.BlockSpec(memory_space=pl.ANY)] * len(kept),
        out_specs=pl.BlockSpec((block, width), lambda i: (first + i, 0)),
        out_shape=jax.ShapeDtypeStruct((total, width), BF16),
        input_output_aliases={2: 0} if kept else {},
        compiler_params=params(),
        name="pack",
    )(target_row, rows, *kept)


def unpack_rows(target, refs):
    base = 0
    picked = None
    for ref in refs:
        count = ref.shape[0]
        hot = iota((target.shape[0], count), 1) + base == target
        part = dot(jnp.where(hot, 1.0, 0.0).astype(BF16), ref[...])
        picked = part if picked is None else picked + part
        base += count
    return picked


def middle_kernel(*refs):
    slots = refs[:CHUNKS]
    tgt_ref, hid_ref, dy_ref, vec_ref, dhid_ref, da_ref, sum_ref = refs[CHUNKS:]
    dmoe = unpack_rows(tgt_ref[...], slots)
    scaled, inverse = norm_stats(hid_ref[...])
    dhid = dy_ref[...].astype(F32) + norm_back(dmoe, scaled, inverse, vec_ref[1:2, :])
    dhid_ref[...] = dhid
    low = dhid.astype(BF16)
    da_ref[...] = low

    @pl.when(pl.program_id(0) == 0)
    def _():
        sum_ref[...] = jnp.zeros_like(sum_ref)

    sum_ref[0:1, :] += jnp.sum(low.astype(F32), axis=0, keepdims=True)
    sum_ref[1:2, :] += jnp.sum(dmoe * scaled, axis=0, keepdims=True)
    sum_ref[2:3, :] += jnp.sum(dmoe, axis=0, keepdims=True)


def middle(slots, target_col, hidden, dy, vecs):
    tokens, width = hidden.shape
    row = lambda n: pl.BlockSpec((QBLOCK, n), lambda i: (i, 0))
    return pl.pallas_call(
        middle_kernel,
        grid=(tokens // QBLOCK,),
        in_specs=[whole(s.shape) for s in slots] + [row(1), row(width), row(width), whole(vecs.shape)],
        out_specs=(row(width), row(width), whole((8, width))),
        out_shape=(
            jax.ShapeDtypeStruct((tokens, width), F32),
            jax.ShapeDtypeStruct((tokens, width), BF16),
            jax.ShapeDtypeStruct((8, width), F32),
        ),
        compiler_params=params(),
        name="middle",
    )(*slots, target_col, hidden, dy, vecs)


def output_kernel(capacity, slots_ref, tgt_ref, hid_ref, moe_ref, router_ref, out_ref):
    logits = dot(moe_ref[...], router_ref[...])
    past = tgt_ref[...] - iota(logits.shape, 1) * capacity
    chosen = jnp.sum(
        jnp.where((past >= 0) & (past < capacity), logits, 0.0), axis=1, keepdims=True
    )
    gate = jax.nn.sigmoid(chosen)
    out_ref[...] = (hid_ref[...] + gate * unpack_rows(tgt_ref[...], [slots_ref])).astype(BF16)


def finish_output(slots, capacity, target_col, hidden, moe_in, weights, at, count):
    tokens, width = hidden.shape
    row = lambda n: pl.BlockSpec((QBLOCK, n), lambda i: (i, 0))
    return pl.pallas_call(
        functools.partial(output_kernel, capacity),
        grid=(tokens // QBLOCK,),
        in_specs=[
            whole(slots.shape),
            row(1),
            row(width),
            row(width),
            pl.BlockSpec((width, count), lambda i: (0, at // count)),
        ],
        out_specs=row(width),
        out_shape=jax.ShapeDtypeStruct((tokens, width), BF16),
        compiler_params=params(),
        name="finish",
    )(slots, target_col, hidden, moe_in, weights)


def expert_kernel(aliased, *refs):
    x_ref, dy_ref, wi_ref, bi_ref, wo_ref, vec_ref = refs[:6]
    refs = refs[6 + aliased :]
    ret_ref, dmoe_ref, act_ref, dpre_ref, arr_ref, xall_ref, gbi_ref, sum_ref = refs[:8]
    accr_ref, accg_ref = refs[8:]
    step = pl.program_id(0)

    def gate_of():
        x = x_ref[...].astype(F32)
        return jax.nn.sigmoid(jnp.sum(x * vec_ref[1:2, :], axis=1, keepdims=True))

    @pl.when(step == 0)
    def _():
        arr_ref[...] = (dy_ref[...].astype(F32) * gate_of()).astype(BF16)
        xall_ref[...] = x_ref[...]
        accr_ref[...] = jnp.broadcast_to(vec_ref[0:1, :], accr_ref.shape)
        accg_ref[...] = jnp.zeros_like(accg_ref)

    pre = dot(x_ref[...], wi_ref[...]) + bi_ref[...]
    dact = dot_nt(arr_ref[...], wo_ref[...])
    phi = 0.5 * (1.0 + lax.erf(pre * SQRT_HALF))
    act = (pre * phi).astype(BF16)
    act_ref[...] = act
    accr_ref[...] += dot(act, wo_ref[...])
    slope = phi + pre * jnp.exp(-0.5 * pre * pre) * INV_ROOT_TAU
    dpre = (dact * slope).astype(BF16)
    dpre_ref[...] = dpre
    accg_ref[...] += dot_nt(dpre, wi_ref[...])
    gbi_ref[...] = jnp.broadcast_to(
        jnp.sum(dpre.astype(F32), axis=0, keepdims=True), gbi_ref.shape
    )

    @pl.when(step == pl.num_programs(0) - 1)
    def _():
        gate = gate_of()
        ret = accr_ref[...].astype(BF16)
        ret_ref[...] = ret
        dgate = jnp.sum(dy_ref[...].astype(F32) * ret.astype(F32), axis=1, keepdims=True)
        dlogit = (dgate * gate * (1.0 - gate)).astype(BF16).astype(F32)
        dmoe_ref[...] = (
            accg_ref[...].astype(BF16).astype(F32) + dlogit * vec_ref[1:2, :]
        ).astype(BF16)
        sum_ref[...] = jnp.zeros_like(sum_ref)
        sum_ref[0:1, :] = jnp.sum(x_ref[...].astype(F32) * dlogit, axis=0, keepdims=True)
        sum_ref[1:2, :] = jnp.sum(arr_ref[...].astype(F32), axis=0, keepdims=True)


def expert_chunk(chunk, total, x, dy, w_in, b_in, w_out, vecs, kept):
    rows, width = x.shape
    hidden = w_in.shape[1]
    block = 512
    aliased = len(kept)
    any_spec = pl.BlockSpec(memory_space=pl.ANY)
    return pl.pallas_call(
        functools.partial(expert_kernel, aliased),
        grid=(hidden // block,),
        in_specs=[
            whole(x.shape),
            whole(dy.shape),
            pl.BlockSpec((width, block), lambda f: (0, f)),
            pl.BlockSpec((1, block), lambda f: (0, f)),
            pl.BlockSpec((block, width), lambda f: (f, 0)),
            whole(vecs.shape),
        ]
        + [any_spec] * aliased,
        out_specs=(
            whole((rows, width)),
            whole((rows, width)),
            pl.BlockSpec((rows, block), lambda f: (chunk, f)),
            pl.BlockSpec((rows, block), lambda f: (chunk, f)),
            pl.BlockSpec((rows, width), lambda f: (chunk, 0)),
            pl.BlockSpec((rows, width), lambda f: (chunk, 0)),
            pl.BlockSpec((8, block), lambda f: (0, f)),
            whole((8, width)),
        ),
        out_shape=(
            jax.ShapeDtypeStruct((rows, width), BF16),
            jax.ShapeDtypeStruct((rows, width), BF16),
            jax.ShapeDtypeStruct((total, hidden), BF16),
            jax.ShapeDtypeStruct((total, hidden), BF16),
            jax.ShapeDtypeStruct((total, width), BF16),
            jax.ShapeDtypeStruct((total, width), BF16),
            jax.ShapeDtypeStruct((8, hidden), F32),
            jax.ShapeDtypeStruct((8, width), F32),
        ),
        scratch_shapes=[pltpu.VMEM((rows, width), F32), pltpu.VMEM((rows, width), F32)],
        input_output_aliases={6 + i: 2 + i for i in range(aliased)},
        compiler_params=params(),
        name="expert",
    )(x, dy, w_in, b_in, w_out, vecs, *kept)


def levels_of(devices):
    side = int(round((devices // 8) ** 0.5))
    return (devices // (2 * side * side), side, side, 2)


def cyclic(devices, sizes, axis, shift):
    stride = 1
    for size in sizes[axis + 1 :]:
        stride *= size
    pairs = []
    for i in range(devices):
        at = (i // stride) % sizes[axis]
        pairs.append((i, i + ((at + shift) % sizes[axis] - at) * stride))
    return pairs


def coordinate(sizes, axis):
    stride = 1
    for size in sizes[axis + 1 :]:
        stride *= size
    return lax.rem(lax.div(lax.axis_index("dp"), stride), sizes[axis])


def shifted(block, devices, sizes, axis):
    parts = [block]
    for shift in range(1, sizes[axis]):
        parts.append(lax.ppermute(block, "dp", cyclic(devices, sizes, axis, shift)))
    return parts


def in_order(parts, mine, position):
    size = len(parts)
    slots = []
    for j in range(size):
        back = lax.rem(mine + (size - j), size)
        slot = parts[0]
        for shift in range(1, size):
            slot = jnp.where(back == shift, parts[shift], slot)
        slots.append(slot)
    return jnp.stack(slots, axis=position)


def gather_level(block, devices, sizes, axis, position):
    return in_order(shifted(block, devices, sizes, axis), coordinate(sizes, axis), position)


def gather_rows(block, devices):
    sizes = levels_of(devices)
    rows, width = block.shape
    cut = (width // 256) * 128
    block = gather_level(block, devices, sizes, 0, 0)
    first, second = block[..., :cut], block[..., cut:]
    first = gather_level(first, devices, sizes, 1, 1)
    second = gather_level(second, devices, sizes, 2, 1)
    first = gather_level(first, devices, sizes, 2, 2)
    second = gather_level(second, devices, sizes, 1, 1)
    both = jnp.concatenate([first, second], axis=-1)
    both = gather_level(both, devices, sizes, 3, 3)
    return both.reshape(devices * rows, width)


def scatter_level(blocks, devices, sizes, axis, position):
    size = sizes[axis]
    mine = coordinate(sizes, axis)
    totals = [lax.dynamic_index_in_dim(block, mine, position, keepdims=False) for block in blocks]
    for shift in range(1, size):
        other = lax.rem(mine + shift, size)
        parts = [
            lax.dynamic_index_in_dim(block, other, position, keepdims=False).astype(BF16) for block in blocks
        ]
        part = jnp.concatenate(parts, axis=-1) if len(parts) > 1 else parts[0]
        got = lax.ppermute(part, "dp", cyclic(devices, sizes, axis, shift))
        base = 0
        for n, total in enumerate(totals):
            width = total.shape[-1]
            totals[n] = total + got[..., base : base + width].astype(F32)
            base += width
    return totals


def scatter_rows(parts, own, devices):
    sizes = levels_of(devices)
    got = lax.ppermute(parts, "dp", cyclic(devices, sizes, 3, 1))
    shape = sizes[:3] + (parts.shape[0] * 2 // devices,)
    half = parts.shape[1] // 2
    first, second = (
        [(own[:, cut] + got[:, cut].astype(F32)).reshape(shape + (half,))]
        for cut in (slice(0, half), slice(half, 2 * half))
    )
    first = scatter_level(first, devices, sizes, 2, 2)
    second = scatter_level(second, devices, sizes, 1, 1)
    first = scatter_level(first, devices, sizes, 1, 1)
    second = scatter_level(second, devices, sizes, 2, 1)
    return scatter_level(first + second, devices, sizes, 0, 0)


def other_first(rows, devices):
    place = coordinate(levels_of(devices), 3)
    split = rows.reshape(devices // 2, 2, rows.shape[0] // devices, rows.shape[1])
    pick = lambda index: lax.dynamic_index_in_dim(split, index, 1, keepdims=False)
    return jnp.concatenate([pick(1 - place), pick(place)], axis=0).reshape(rows.shape)


def exchange(slots, experts):
    rows, width = slots.shape
    out = lax.all_to_all(slots.reshape(experts, rows // experts, width), "dp", split_axis=0, concat_axis=0, tiled=True)
    return out.reshape(rows, width)


def per_device(
    inputs,
    cotangent,
    routes,
    segments,
    qkv_weight,
    query_bias,
    value_bias,
    out_weight,
    out_bias,
    attn_gain,
    attn_shift,
    moe_gain,
    moe_shift,
    router_weight,
    expert_in,
    expert_in_bias,
    expert_out,
    expert_out_bias,
):
    seq_count, tokens, width = inputs.shape
    devices = lax.axis_size("dp")
    experts = router_weight.shape[1]
    capacity = 2 * tokens // devices
    per_chunk = capacity // CHUNKS
    chunk_rows = experts * per_chunk
    wide = width // GROUPS
    rows = qkv_weight.shape[0]
    x = inputs.reshape(tokens, width)
    dy = cotangent.reshape(tokens, width)

    blocks = qkv_weight.reshape(rows, 3, GROUPS, wide).transpose(0, 2, 1, 3)
    blocks = blocks.reshape(rows, GROUPS, 3 * wide).astype(BF16)
    early = jnp.stack([attn_gain, attn_shift, query_bias, value_bias], axis=1).astype(BF16)
    early = jnp.pad(early, ((0, 0), (0, 128 - early.shape[1])))
    late = jnp.concatenate(
        [router_weight, out_bias[:, None], moe_gain[:, None], moe_shift[:, None]], axis=1
    ).astype(BF16)
    late = jnp.pad(late, ((0, 0), (0, -late.shape[1] % 128)))
    full = gather_rows(
        jnp.concatenate([blocks.reshape(rows, 3 * width), out_weight.astype(BF16), late, early], axis=1), devices
    )
    router_at, router_wide = 4 * width, late.shape[1]
    early_rows = full[:, router_at + router_wide :][:, :8].astype(F32).T
    late_rows = full[:, router_at : router_at + router_wide].astype(F32).T
    vecs = jnp.pad(late_rows[experts : experts + 3], ((0, 5), (0, 0)))
    router_row = lax.dynamic_index_in_dim(late_rows, lax.axis_index("dp"), 0, keepdims=True)

    route = routes.reshape(tokens)
    onehot = route[:, None] == jnp.arange(experts, dtype=jnp.int32)[None, :]
    place = jnp.arange(tokens, dtype=jnp.int32)
    earlier = jnp.dot(
        (place[None, :] < place[:, None]).astype(BF16),
        onehot.astype(BF16),
        preferred_element_type=F32,
    )
    slot = jnp.sum(jnp.where(onehot, earlier, 0.0), axis=1).astype(jnp.int32)

    def places_of(route, slot):
        chunk = sum(jnp.where(slot >= n * per_chunk, 1, 0) for n in range(1, CHUNKS))
        return chunk * (chunk_rows - per_chunk) + route * per_chunk + slot, route * capacity + slot

    target_row, entire_row = places_of(route[None, :], slot[None, :])
    target_col, entire_col = places_of(route[:, None], slot[:, None])

    slots = CHUNKS * chunk_rows
    dy_slots = ()
    for c in range(CHUNKS):
        dy_slots = (
            pack(dy, entire_row, c * chunk_rows, chunk_rows, slots, dy_slots),
        )
    dy_slots = exchange(dy_slots[0], experts).reshape(experts, CHUNKS, per_chunk, width)
    dys = [dy_slots[:, c].reshape(chunk_rows, width) for c in range(CHUNKS)]
    w_in = expert_in[0].astype(BF16)
    w_out = expert_out[0].astype(BF16)

    seg_row = segments.reshape(1, tokens)
    seg_col = segments.reshape(tokens, 1)
    scaled, _ = norm_stats(x.astype(F32))
    normed = (scaled * early_rows[0:1] + early_rows[1:2]).astype(BF16)
    qkv, mix, lse = attend(normed, full, early_rows, seg_col, seg_row)
    hidden, moe_in = project(x, mix, full, vecs)

    expert_vecs = jnp.concatenate([expert_out_bias, router_row, jnp.zeros((6, width), F32)], axis=0)
    returned, dmoes, kept = [], [], ()
    dbias_in = dsums = 0.0
    received = [
        exchange(pack(moe_in, target_row, c * chunk_rows, chunk_rows, chunk_rows), experts)
        for c in range(CHUNKS)
    ]
    mix_t = other_first(mix.T, devices)
    normed_t = other_first(normed.T, devices)
    received[0], target_col, entire_col, mix_t, normed_t = lax.optimization_barrier(
        (received[0], target_col, entire_col, mix_t, normed_t)
    )
    for c in range(CHUNKS):
        ret, dmoe, *kept, dbias, sums = expert_chunk(
            c, CHUNKS * chunk_rows, received[c], dys[c], w_in, expert_in_bias, w_out, expert_vecs, kept
        )
        dmoes.append(exchange(dmoe, experts))
        returned.append(ret)
        dbias_in = dbias_in + dbias[0:1]
        dsums = dsums + sums
    act, dpre, arrived, rows_in = kept
    grad_expert_out = dot_tn(act, arrived)
    grad_expert_in = dot_tn(rows_in, dpre)
    returned = jnp.stack([r.reshape(experts, per_chunk, width) for r in returned], axis=1)
    returned = exchange(returned.reshape(slots, width), experts)

    dhid, dattn, mid_sums = middle(dmoes, target_col, hidden, dy, vecs)
    qkv_sums, parts, own, grad_inputs, last_sums = behind(
        qkv, mix, dattn, full, lse, seg_col, seg_row, normed_t, mix_t, early_rows, x, dhid
    )
    grads = jnp.concatenate(scatter_rows(parts, own, devices), axis=1)
    grad_qkv, grad_out = grads[:, : 3 * width], grads[:, 3 * width :]
    output = finish_output(
        returned, capacity, entire_col, hidden, moe_in, full, router_at, router_wide
    )

    qkv_sums = qkv_sums[0].reshape(GROUPS, 3, wide)
    grad_query, grad_value = qkv_sums[:, 0].reshape(1, width), qkv_sums[:, 2].reshape(1, width)
    small = jnp.concatenate([grad_query, grad_value, mid_sums[0:3], last_sums[0:2], dsums[0:1]], axis=0)
    small = small.reshape(8, devices, rows).transpose(1, 0, 2).reshape(devices, 8 * rows)
    small = jnp.pad(small, ((0, 0), (0, -small.shape[1] % 128)))
    small = lax.all_to_all(small, "dp", split_axis=0, concat_axis=0, tiled=True)
    vectors = jnp.sum(small[:, : 7 * rows], axis=0).reshape(7, rows)
    grad_router = small[:, 7 * rows : 8 * rows].T
    grad_qkv = grad_qkv.reshape(rows, GROUPS, 3, wide).transpose(0, 2, 1, 3).reshape(rows, 3 * width)
    return (
        output.reshape(seq_count, tokens, width),
        grad_inputs.reshape(seq_count, tokens, width),
        grad_qkv,
        vectors[0],
        vectors[1],
        grad_out,
        vectors[2],
        vectors[5],
        vectors[6],
        vectors[3],
        vectors[4],
        grad_router,
        grad_expert_in[None],
        dbias_in,
        grad_expert_out[None],
        dsums[1:2],
    )


def solution(mesh):
    placed = (
        P("dp", None, None),
        P("dp", None, None),
        P("dp", None, None),
        P("dp", None),
        P("dp", None),
        P("dp"),
        P("dp"),
        P("dp", None),
        P("dp"),
        P("dp"),
        P("dp"),
        P("dp"),
        P("dp"),
        P("dp", None),
        P("dp", None, None),
        P("dp", None),
        P("dp", None, None),
        P("dp", None),
    )
    return jax.shard_map(
        per_device,
        mesh=mesh,
        in_specs=placed,
        out_specs=(
            P("dp", None, None),
            P("dp", None, None),
            P("dp", None),
            P("dp"),
            P("dp"),
            P("dp", None),
            P("dp"),
            P("dp"),
            P("dp"),
            P("dp"),
            P("dp"),
            P("dp", None),
            P("dp", None, None),
            P("dp", None),
            P("dp", None, None),
            P("dp", None),
        ),
        check_vma=False,
    )
```
